32 devices in a mesh: cond: 4 (over z), ty: 2 (over y), tx: 4 (over x, core).
Axes of the slice: x: 2, y: 2, z: 4, core: 2. Of those that a mesh axis runs over, the one named last changes fastest.
Arguments:
- mask_logits: float32 [1024, 2048], P('ty', 'tx'), may hold values from -8 to 8
- target_layout: int32 [1024, 2048], P('ty', 'tx'), may hold values 0 or 1
- density_weights: int32 [1024, 2048], P('ty', 'tx'), may hold values from 0 to 3, as said below
- socs_kernels: float32 [4, 12, 2, 24, 24], P('cond'), may hold values from -3 to 3
Outputs:
- logits_new: float32 [1024, 2048], P('ty', 'tx')
- mask_next: bfloat16 [1024, 2048], P('ty', 'tx')
The draws below stay inside these ranges and needn't reach their ends.
Inputs may be any that keep to these rules, and one draw needn't show every extreme that they name: `density_weights`: weights are constant zero over exactly a quarter, rounded down, of the 512 x 512 tiles; elsewhere each pixel's weight is drawn afresh.
All inputs are finite; a program needn't handle non-finite values. No bound on the sum of `target_layout` on one device may be relied on, other than what follows from the above.
Results may differ from the reference program's by a relative error of at most 0.001.
Values sent between devices are 32-bit elements; how exact they have to be, the bound alone decides.
A program may use at most 64 MiB of HBM per device.

```python
import math
import jax
import jax.numpy as jnp
from jax import lax

TILE = 512
MARGIN = 128
BAND = 24
KERN = 12
COND = 4
ROWS = 1024
COLS = 2048
N_TY = 2
N_TX = 4


def draw_density_weights(key, part):
    key_rank, key_level = jax.random.split(jax.random.fold_in(key, 11))
    tiles_down = ROWS // TILE
    tiles_across = COLS // TILE
    tile_count = tiles_down * tiles_across
    ranking = jax.random.permutation(key_rank, tile_count)
    active = (ranking >= tile_count // 4).astype(jnp.int32).reshape(tiles_down, 1, tiles_across, 1)
    levels = jax.random.randint(key_level, (tiles_down, TILE, tiles_across, TILE), 0, 4, dtype=jnp.int32)
    return (levels * active).reshape(ROWS, COLS)


def set_ends(drawn, own_key, smallest, largest):
    dims = drawn.shape
    place = [jax.random.randint(jax.random.fold_in(own_key, axis), (), 0, dims[axis]) for axis in range(len(dims))]
    drawn = drawn.at[tuple(place)].set(smallest)
    longest = dims.index(max(dims))
    place[longest] = (place[longest] + 1) % dims[longest]
    return drawn.at[tuple(place)].set(largest)


def shard_levels(rng, extent, cuts, least, high):
    gain = 1.0
    for dim, blocks in cuts:
        steps = jax.random.uniform(jax.random.fold_in(jax.random.fold_in(rng, 6), dim), (blocks,), jnp.float32, least / len(cuts), high / len(cuts))
        gain = gain * jnp.repeat(jnp.exp(steps), extent[dim] // blocks).reshape((-1,) + (1,) * (len(extent) - 1 - dim))
    return gain


def noise(stream_key, shape, scale, most, cuts=(), kind=jnp.bfloat16):
    entries = jax.random.normal(stream_key, shape, jnp.float32) * scale
    if len(cuts) > 0:
        entries = shard_levels(stream_key, shape, cuts, -0.22, 0.18) * entries
    return jnp.clip(entries, min=-most, max=most).astype(kind)


def setup_inputs(seed: int = 0) -> dict:
    seeds = jax.random.split(jax.random.key(seed), 5)
    mask_logits = noise(seeds[0], (ROWS, COLS), 1.5, 8.0, ((0, 2), (1, 4)), jnp.float32)
    target_layout = set_ends((jax.random.randint(seeds[1], (ROWS, COLS), 0, 5) < 2).astype(jnp.int32), jax.random.fold_in(seeds[1], 1), 0, 1)
    density_weights = draw_density_weights(jax.random.fold_in(seeds[4], 71), 0)
    socs_kernels = noise(seeds[3], (COND, KERN, 2, BAND, BAND), ((2 * KERN) ** -0.5), 3.0, ((0, 4),), jnp.float32)
    return dict(mask_logits=mask_logits, target_layout=target_layout, density_weights=density_weights, socs_kernels=socs_kernels)


STEEPNESS = 6.0
THRESHOLD = 0.25
STEP_SIZE = 4.0

def matmul_hi(first, second):
    return jnp.dot(first, second, precision=lax.Precision.HIGHEST, preferred_element_type=jnp.float32)

def band_tables(count_rows, offset, length, band_size):
    positions = jnp.arange(count_rows, dtype=jnp.int32) + offset
    frequency = jnp.arange(band_size, dtype=jnp.int32) - band_size // 2
    turn_count = jnp.mod(positions[:, None] * frequency[None, :], length).astype(jnp.float32)
    angles = turn_count * (2.0 * math.pi / length)
    return (jnp.cos(angles), jnp.sin(angles))

def tile_loss(window, layout, weight_vals, kernels_here):
    length = window.shape[0]
    win_cos, win_sin = band_tables(length, 0, length, BAND)
    tile_cos, tile_sin = band_tables(TILE, MARGIN, length, BAND)
    normalizer = 1.0 / (length * length)
    cos_rows = matmul_hi(win_cos.T, window)
    sin_rows = matmul_hi(win_sin.T, window)
    spec_re = (matmul_hi(cos_rows, win_cos) - matmul_hi(sin_rows, win_sin)) * normalizer
    spec_im = -(matmul_hi(cos_rows, win_sin) + matmul_hi(sin_rows, win_cos)) * normalizer
    intensity = jnp.zeros((TILE, TILE), jnp.float32)
    for kernel_index in range(KERN):
        kern_re = kernels_here[kernel_index, 0]
        kern_im = kernels_here[kernel_index, 1]
        amp_re = kern_re * spec_re - kern_im * spec_im
        amp_im = kern_re * spec_im + kern_im * spec_re
        half_re = matmul_hi(amp_re, tile_cos.T) - matmul_hi(amp_im, tile_sin.T)
        half_im = matmul_hi(amp_re, tile_sin.T) + matmul_hi(amp_im, tile_cos.T)
        field_re = matmul_hi(tile_cos, half_re) - matmul_hi(tile_sin, half_im)
        field_im = matmul_hi(tile_cos, half_im) + matmul_hi(tile_sin, half_re)
        intensity = intensity + field_re * field_re + field_im * field_im
    resist = jax.nn.sigmoid(STEEPNESS * (intensity - THRESHOLD))
    return jnp.sum(weight_vals * (resist - layout) ** 2)

def reference(mask_logits, target_layout, density_weights, socs_kernels):
    mask_now = 0.5 * (1.0 + jnp.tanh(mask_logits))
    padded = jnp.pad(mask_now, MARGIN)
    length = TILE + 2 * MARGIN
    tile_count = N_TY * N_TX

    def visit_tile(accumulated, tile_index):
        row_start = tile_index // N_TX * TILE
        col_start = tile_index % N_TX * TILE
        window = lax.dynamic_slice(padded, (row_start, col_start), (length, length))
        layout = lax.dynamic_slice(target_layout, (row_start, col_start), (TILE, TILE)).astype(jnp.float32)
        weight_vals = lax.dynamic_slice(density_weights, (row_start, col_start), (TILE, TILE)).astype(jnp.float32)
        window_grad = jnp.zeros((length, length), jnp.float32)
        for condition in range(COND):
            window_grad = window_grad + jax.grad(tile_loss)(window, layout, weight_vals, socs_kernels[condition])
        previous = lax.dynamic_slice(accumulated, (row_start, col_start), (length, length))
        return (lax.dynamic_update_slice(accumulated, previous + window_grad, (row_start, col_start)), None)
    accumulated, _ = lax.scan(visit_tile, jnp.zeros_like(padded), jnp.arange(tile_count, dtype=jnp.int32))
    mask_grad = accumulated[MARGIN:MARGIN + ROWS, MARGIN:MARGIN + COLS]
    logits_new = mask_logits - STEP_SIZE * mask_grad * (2.0 * mask_now * (1.0 - mask_now))
    mask_next = (0.5 * (1.0 + jnp.tanh(logits_new))).astype(jnp.bfloat16)
    return (logits_new, mask_next)
```

```python
import functools
import math

import jax
import jax.numpy as jnp
import numpy as np
from jax import lax
from jax.experimental import pallas as pl
from jax.experimental.pallas import tpu as pltpu
from jax.sharding import PartitionSpec as P

MARGIN = 128
STEEPNESS = 6.0
THRESHOLD = 0.25
STEP_SIZE = 4.0
LANES = 128
HALF = 16
SLOT = 2 * HALF
SLOTS = LANES // SLOT
WIDE = 64
MESH = pl.DeviceIdType.MESH
OFFSETS = [(dr, dc) for dr in (-1, 0, 1) for dc in (-1, 0, 1)]
BF = jnp.bfloat16
F32 = jnp.float32


def halves(table):
    table = np.asarray(table, np.float32)
    high = table.astype(BF)
    return high, (table - high.astype(np.float32)).astype(BF)


def place(rows, cols, *pieces):
    out = np.zeros((rows, cols))
    for top, left, piece in pieces:
        out[top : top + piece.shape[0], left : left + piece.shape[1]] = piece
    return out


def trig(positions, top, period):
    turns = np.mod(np.outer(positions, np.arange(top + 1)), period).astype(np.float64)
    angle = turns * (2 * math.pi / period)
    return place(len(positions), SLOT, (0, 0, np.cos(angle)), (0, HALF, np.sin(angle)))


def make_tables(tile, margin, band):
    top = band // 2
    assert band % 2 == 0 and top < HALF and tile >= 2 * margin
    length = tile + 2 * margin
    grid = -(-(2 * band - 1) // 16) * 16
    assert grid <= WIDE
    shifted = []
    for step in (-1, 0, 1):
        spots = np.arange(tile) + margin - step * tile
        inside = ((spots >= 0) & (spots < length))[:, None]
        shifted.append(trig(spots, top, length) * inside)
    wave = np.concatenate(shifted, 1)
    fh, fl = halves(wave)
    pad = np.zeros((tile, LANES - 3 * SLOT), fh.dtype)
    fcol = np.concatenate([fh, pad, fl, pad], 1)
    frow = np.concatenate([fh.T, fl.T], 0)

    ec = trig(np.arange(grid), top, grid)
    bh, bl = halves(ec)
    norm = 1.0 / (length * length)
    sh, sl = halves(ec * norm)
    block = place(LANES, SLOTS * WIDE, *((SLOT * j, WIDE * j, ec.T) for j in range(SLOTS)))
    th, tl = halves(block)
    turn = (np.arange(tile) + margin)[:, None] / length - np.arange(grid)[None, :] / grid
    orders = np.arange(1, band)
    interp = (1 + 2 * np.cos(2 * math.pi * turn[:, :, None] * orders).sum(-1)) / grid
    ih, il = halves(interp)
    gap = np.zeros((tile, WIDE - grid), ih.dtype)
    wn = np.concatenate([ih, gap, ih, gap, il, gap, il, gap], 1)
    wt = np.concatenate([ih.T, il.T], 0)

    plus, minus = np.zeros((HALF, band)), np.zeros((HALF, band))
    for m in range(top):
        plus[m, top + m] = 1
    for m in range(1, top + 1):
        minus[m, top - m] = 1
    even, odd = plus + minus, plus - minus
    kl = np.concatenate([even, even, -odd, odd], 0)
    kr = np.stack([
        place(
            band, 2 * LANES,
            (0, SLOT * j, even.T), (0, SLOT * j + HALF, even.T),
            (0, LANES + SLOT * j, -odd.T), (0, LANES + SLOT * j + HALF, odd.T),
        )
        for j in range(SLOTS)
    ])
    front = dict(
        fcol=fcol, frow=frow, kr=kr.astype(BF), kl=kl.astype(BF),
        left=np.concatenate([sh, sh, sl], 1),
        th=th, tl=tl, wt=wt, wn=wn,
        tb=np.concatenate([th.T, tl.T], 1),
        lt=np.concatenate([bh.T, bh.T, bl.T], 1),
    )
    edge, mid = [0, SLOT], [SLOT, 2 * SLOT]
    rows = np.zeros((tile, 6 * SLOT), fh.dtype)
    for lo, hi, cut in ((0, margin, 0), (tile - margin, tile, SLOT)):
        pick = slice(cut, cut + 2 * SLOT)
        rows[lo:hi] = np.concatenate([fh[lo:hi, pick], fh[lo:hi, pick], fl[lo:hi, pick]], 1)
    lo, hi, pick = margin, tile - margin, slice(SLOT, 2 * SLOT)
    rows[lo:hi, : 3 * SLOT] = np.concatenate([fh[lo:hi, pick], fh[lo:hi, pick], fl[lo:hi, pick]], 1)
    back = dict(frow=frow, brow=rows)
    return front, back, grid


def split(x):
    high = x.astype(BF)
    return high, (x - high.astype(F32)).astype(BF)


def mm(a, b):
    return jnp.dot(a, b, preferred_element_type=F32)


def roll(x, shift):
    shift = shift % LANES
    return x if shift == 0 else pltpu.roll(x, shift, 1)


def by_slot(pieces):
    lane = lax.broadcasted_iota(jnp.int32, pieces[0].shape, 1)
    out = pieces[-1]
    for j in range(len(pieces) - 2, -1, -1):
        out = jnp.where(lane < (j + 1) * SLOT, pieces[j], out)
    return out


def swap(x):
    return jnp.concatenate([x[HALF:], x[:HALF]], 0)


def front_kernel(names, grid, n_k, *refs):
    n_tab = len(names)
    logits_hbm, target_hbm, weight_hbm, kern_hbm = refs[:4]
    tab_hbm = dict(zip(names, refs[4 : 4 + n_tab]))
    late_hbm = refs[4 + n_tab]
    out_ref, logits, fac, frow, late = refs[5 + n_tab : 10 + n_tab]
    rest = refs[10 + n_tab :]
    target, weight, kern = rest[:3]
    own = [n for n in names if n != "frow"]
    tab = dict(zip(own, rest[3 : 3 + len(own)]), frow=frow)
    (kq, send1, recv1, zs_own, recv_c, zs_sum, recv2, level, signed,
     load_sem, s1, r1, sc, rc, s2, r2) = rest[3 + len(own) :]

    tile = logits.shape[0]
    band = kern.shape[-1]
    n_g = n_k // SLOTS
    length = tile + 2 * MARGIN
    norm = 1.0 / (length * length)
    chunk = min(tile, 128)
    parts = [slice(i, i + chunk) for i in range(0, tile, chunk)]
    n_ty, n_tx, n_c = lax.axis_size("ty"), lax.axis_size("tx"), lax.axis_size("cond")
    ty, tx, me = lax.axis_index("ty"), lax.axis_index("tx"), lax.axis_index("cond")

    jobs = [("fcol", tab_hbm["fcol"], tab["fcol"])]
    jobs += [(part.start, logits_hbm.at[part], logits.at[part]) for part in parts]
    jobs += [("frow", tab_hbm["frow"], frow), ("kern", kern_hbm, kern)]
    jobs += [(n, tab_hbm[n], tab[n]) for n in ("kr", "kl")]
    jobs += [("target", target_hbm, target), ("weight", weight_hbm, weight)]
    jobs += [(n, tab_hbm[n], tab[n]) for n in own if n not in ("fcol", "kr", "kl")]
    jobs += [("late", late_hbm, late)]
    loads = {}
    for i, (name, source, dest) in enumerate(jobs):
        loads[name] = pltpu.make_async_copy(source, dest, load_sem.at[i])
        loads[name].start()

    def exists(dr, dc):
        row, col = ty + dr, tx + dc
        return (row >= 0) & (row < n_ty) & (col >= 0) & (col < n_tx)

    around = [(i, o) for i, o in enumerate(OFFSETS) if o != (0, 0)]
    barrier = pltpu.get_barrier_semaphore()
    for _, (dr, dc) in around:
        @pl.when(exists(dr, dc))
        def _():
            pl.semaphore_signal(
                barrier, inc=1, device_id={"ty": ty + dr, "tx": tx + dc}, device_id_type=MESH
            )
    for j in range(1, n_c):
        pl.semaphore_signal(
            barrier, inc=1, device_id={"cond": lax.rem(me + j, n_c)}, device_id_type=MESH
        )
    for i, (dr, dc) in around:
        @pl.when(jnp.logical_not(exists(-dr, -dc)))
        def _():
            recv1[i] = jnp.zeros(recv1.shape[1:], F32)
            recv2[i] = jnp.zeros(recv2.shape[1:], F32)

    loads["fcol"].wait()
    share = None
    for i, part in enumerate(parts):
        loads[part.start].wait()
        mh, ml = split(0.5 + 0.5 * jnp.tanh(logits[part]))
        both = mm(mh, tab["fcol"][...])
        proj = both[:, :LANES] + both[:, LANES:] + mm(ml, tab["fcol"][:, :LANES])
        if i == 0:
            loads["frow"].wait()
        piece = mm(frow[:, part], jnp.concatenate(split(proj), 1))
        share = piece if share is None else share + piece
    n_f = 3 * SLOT
    share = share[:n_f, :LANES] + share[:n_f, LANES:] + share[n_f:, :LANES]
    for i, (dr, dc) in enumerate(OFFSETS):
        top = (dr + 1) * SLOT
        send1[i] = by_slot(
            [roll(share[top + 8 * t : top + 8 * t + 8], SLOT * (t - dc - 1)) for t in range(SLOTS)]
        )

    peers = n_c - 1
    for _, (dr, dc) in around:
        peers = peers + exists(dr, dc).astype(jnp.int32)
    pl.semaphore_wait(barrier, peers)

    def to_neighbour(source, dest, ss, rs, i, dr, dc):
        return pltpu.make_async_remote_copy(
            src_ref=source, dst_ref=dest.at[i], send_sem=ss.at[i], recv_sem=rs.at[i],
            device_id={"ty": ty + dr, "tx": tx + dc}, device_id_type=MESH,
        )

    far = sorted(around, key=lambda e: -abs(e[1][0]) - abs(e[1][1]))
    for i, (dr, dc) in far:
        @pl.when(exists(dr, dc))
        def _():
            to_neighbour(send1.at[i], recv1, s1, r1, i, dr, dc).start()

    for name in ("kern", "kr", "kl"):
        loads[name].wait()
    turned = None
    for j in range(SLOTS):
        rows = jnp.concatenate(
            [kern[0, SLOTS * g + j, ri] for g in range(n_g) for ri in range(2)], 0
        )
        high, low = split(rows)
        piece = mm(high, tab["kr"][j]) + mm(low, tab["kr"][j])
        turned = piece if turned is None else turned + piece
    for e in range(2 * n_g):
        high, low = split(turned[e * band : (e + 1) * band])
        kq[:, 2 * LANES * e : 2 * LANES * (e + 1)] = mm(tab["kl"][...], high) + mm(tab["kl"][...], low)
    loads["target"].wait()
    loads["weight"].wait()

    def prepare(i, carry):
        part = pl.ds(pl.multiple_of(i * 32, 32), 32)
        vals = weight[part].astype(F32)
        level[part] = vals
        signed[part] = vals * (2.0 * target[part].astype(F32) - 1.0)
        mask = jnp.tanh(logits[part])
        fac[part] = (1.5 * STEP_SIZE * norm) * (mask * mask - 1.0)
        return carry

    lax.fori_loop(0, tile // 32, prepare, 0)
    for name in own:
        if name not in ("fcol", "kr", "kl"):
            loads[name].wait()
    loads["late"].wait()

    spec = send1[4]
    for i, (dr, dc) in around:
        @pl.when(exists(-dr, -dc))
        def _():
            to_neighbour(send1.at[i], recv1, s1, r1, i, dr, dc).wait_recv()
    for i, _ in around:
        spec = spec + recv1[i]

    turns = [roll(spec, SLOT * s) for s in range(SLOTS)]
    u = jnp.concatenate(
        [by_slot([turns[(j - t) % SLOTS] for j in range(SLOTS)]) for t in range(SLOTS)], 0
    )
    v = roll(u, HALF)
    us, vs = swap(u), swap(v)

    def quarter(e, row, col):
        left = 2 * LANES * e + LANES * col
        return kq[SLOT * row : SLOT * (row + 1), left : left + LANES]

    coef = []
    for g in range(n_g):
        r, i = 2 * g, 2 * g + 1
        coef.append(quarter(r, 0, 0) * u - quarter(r, 1, 1) * vs - quarter(i, 1, 0) * us - quarter(i, 0, 1) * v)
        coef.append(quarter(i, 0, 0) * u - quarter(i, 1, 1) * vs + quarter(r, 1, 0) * us + quarter(r, 0, 1) * v)
    n_e = 2 * n_g
    ah, al = split(jnp.concatenate(coef, 1))
    half = mm(tab["left"][...], jnp.concatenate([ah, al, ah], 0))
    hh, hl = split(jnp.concatenate([half[:, LANES * e : LANES * (e + 1)] for e in range(n_e)], 0))
    field = mm(hh, tab["th"][...]) + mm(hl, tab["th"][...]) + mm(hh, tab["tl"][...])
    coarse = jnp.zeros((grid, 2 * LANES), F32)
    for e in range(n_e):
        cut = field[grid * e : grid * (e + 1)]
        coarse = coarse + cut * cut
    coarse = coarse[:, :LANES] + coarse[:, LANES:]
    coarse = (0.5 * STEEPNESS) * (coarse + roll(coarse, WIDE) - THRESHOLD)
    ch, cl = split(coarse[:, :grid])
    wt = tab["wt"]
    uh, ul = split(mm(ch, wt[:grid]) + mm(cl, wt[:grid]) + mm(ch, wt[grid:]))
    gap = jnp.zeros((WIDE - grid, tile), BF)
    ustack = jnp.concatenate([uh, gap, ul, gap, uh, gap, gap, gap, gap, gap], 0)[: 4 * WIDE]

    gsum = None
    for part in parts:
        th = jnp.tanh(mm(tab["wn"][part], ustack))
        gain = (level[part] * th - signed[part]) * (1.0 - th * th)
        gh, gl = split(gain)
        wide = mm(gh, tab["wn"][...])
        y = wide[:, :LANES] + wide[:, LANES:] + mm(gl, tab["wn"][:, :LANES])
        piece = mm(wt[:, part], jnp.concatenate(split(y), 1))
        gsum = piece if gsum is None else gsum + piece
    gcoarse = gsum[:grid, :LANES] + gsum[:grid, LANES:] + gsum[grid:, :LANES]

    gpair = jnp.concatenate([gcoarse, gcoarse], 1)
    dh, dl = split(jnp.concatenate([gpair * field[grid * e : grid * (e + 1)] for e in range(n_e)], 0))
    wide = mm(dh, tab["tb"][...])
    down = wide[:, :LANES] + wide[:, LANES:] + mm(dl, tab["tb"][:, :LANES])
    eh, el = split(jnp.concatenate([down[grid * e : grid * (e + 1)] for e in range(n_e)], 1))
    d = mm(tab["lt"][...], jnp.concatenate([eh, el, eh], 0))
    du = jnp.zeros((SLOT, LANES), F32)
    dus, dv, dvs = du, du, du
    for g in range(n_g):
        r, i = 2 * g, 2 * g + 1
        dr_, di_ = d[:, LANES * r : LANES * (r + 1)], d[:, LANES * i : LANES * (i + 1)]
        du = du + quarter(r, 0, 0) * dr_ + quarter(i, 0, 0) * di_
        dus = dus + quarter(r, 1, 0) * di_ - quarter(i, 1, 0) * dr_
        dv = dv + quarter(r, 0, 1) * di_ - quarter(i, 0, 1) * dr_
        dvs = dvs - quarter(r, 1, 1) * dr_ - quarter(i, 1, 1) * di_
    dx = du + swap(dus) + roll(dv + swap(dvs), HALF)
    x = [dx[8 * t : 8 * t + 8] for t in range(SLOTS)]
    lane = lax.broadcasted_iota(jnp.int32, (8, LANES), 1)
    even, low = (lane // SLOT) % 2 == 0, lane < 2 * SLOT
    pair = [
        jnp.where(even, a, b) + jnp.where(
            even, roll(jnp.where(even, b, a), -SLOT), roll(jnp.where(even, b, a), SLOT)
        )
        for a, b in ((x[0], x[1]), (x[2], x[3]))
    ]
    zs_own[...] = jnp.where(low, pair[0], pair[1]) + roll(jnp.where(low, pair[1], pair[0]), 2 * SLOT)

    over = []
    for j in range(1, n_c):
        copy = pltpu.make_async_remote_copy(
            src_ref=zs_own, dst_ref=recv_c.at[j], send_sem=sc.at[j], recv_sem=rc.at[j],
            device_id={"cond": lax.rem(me + j, n_c)}, device_id_type=MESH,
        )
        copy.start()
        over.append(copy)
    total = zs_own[...]
    for j, copy in enumerate(over):
        copy.wait_recv()
        total = total + recv_c[j + 1]
    zs_sum[...] = total
    for i, (dr, dc) in far:
        @pl.when(exists(dr, dc))
        def _():
            to_neighbour(zs_sum, recv2, s2, r2, i, dr, dc).start()
    recv2[4] = total
    for i, (dr, dc) in around:
        @pl.when(exists(-dr, -dc))
        def _():
            to_neighbour(zs_sum, recv2, s2, r2, i, dr, dc).wait_recv()
    for er in (-1, 0, 1):
        blocks = [recv2[OFFSETS.index((-er, -ec))] for ec in (-1, 0, 1)]
        out_ref[(er + 1) * SLOT : (er + 2) * SLOT] = jnp.concatenate(
            [by_slot([roll(b, SLOT * (i - t)) for i, b in enumerate(blocks)]) for t in range(SLOTS)], 0
        )

    for i, (dr, dc) in around:
        @pl.when(exists(dr, dc))
        def _():
            to_neighbour(send1.at[i], recv1, s1, r1, i, dr, dc).wait_send()
            to_neighbour(zs_sum, recv2, s2, r2, i, dr, dc).wait_send()
    for copy in over:
        copy.wait_send()


def back_kernel(z_ref, logits, fac, frow, brow, new_hbm, next_hbm, new, nxt, sem):
    tile = logits.shape[1]
    n_f = 3 * SLOT
    zh, zl = split(z_ref[:, :n_f])
    w = mm(zh, frow[:n_f]) + mm(zl, frow[:n_f]) + mm(zh, frow[n_f:])
    wh, wl = split(w)

    chunk = min(MARGIN, 128)
    copies = []
    for i in range(tile // chunk):
        lo, hi = i * chunk, (i + 1) * chunk
        part = slice(lo, hi)
        first = 0 if lo < MARGIN else SLOT
        last = 3 * SLOT if hi > tile - MARGIN else 2 * SLOT
        pick = slice(first, last)
        stack = jnp.concatenate([wh[pick], wl[pick], wh[pick]], 0)
        grad = mm(brow[part, : 3 * (last - first)], stack)
        value = logits[part] + fac[part] * grad
        new[part] = value
        nxt[part] = (0.5 + 0.5 * jnp.tanh(value)).astype(BF)
        for j, (buf, out) in enumerate(((new, new_hbm), (nxt, next_hbm))):
            copy = pltpu.make_async_copy(buf.at[part], out.at[part], sem.at[2 * i + j])
            copy.start()
            copies.append(copy)
    for copy in copies:
        copy.wait()


def per_device(mask_logits, target_layout, density_weights, socs_kernels):
    tile = mask_logits.shape[0]
    band = socs_kernels.shape[-1]
    n_k = socs_kernels.shape[1]
    assert n_k % SLOTS == 0
    n_c = lax.axis_size("cond")
    front, back, grid = make_tables(tile, MARGIN, band)
    names = list(front)
    arrays = [mask_logits, target_layout, density_weights, socs_kernels]
    tables = {n: jnp.asarray(front[n]) for n in names}
    late = jnp.asarray(back["brow"])
    in_vmem = pl.BlockSpec(memory_space=pltpu.VMEM)
    in_hbm = pl.BlockSpec(memory_space=pl.ANY)
    vmem = lambda a: pltpu.VMEM(a.shape, a.dtype)
    dma = pltpu.SemaphoreType.DMA
    n_off = len(OFFSETS)
    held = (8, LANES)
    n_load = len(names) + 5 + tile // min(tile, 128)
    operands = arrays + [tables[n] for n in names] + [late]
    kept = pl.pallas_call(
        functools.partial(front_kernel, names, grid, n_k),
        out_shape=[
            pltpu.VMEM((3 * SLOT, LANES), F32), pltpu.VMEM((tile, tile), F32),
            pltpu.VMEM((tile, tile), F32), vmem(tables["frow"]), vmem(late),
        ],
        in_specs=[in_hbm] * len(operands),
        out_specs=[in_vmem] * 5,
        scratch_shapes=[vmem(a) for a in arrays[1:]]
        + [vmem(tables[n]) for n in names if n != "frow"]
        + [
            pltpu.VMEM((2 * SLOT, 2 * LANES * 2 * n_k // SLOTS), F32),
            pltpu.VMEM((n_off, *held), F32),
            pltpu.VMEM((n_off, *held), F32),
            pltpu.VMEM(held, F32),
            pltpu.VMEM((n_c, *held), F32),
            pltpu.VMEM(held, F32),
            pltpu.VMEM((n_off, *held), F32),
            pltpu.VMEM((tile, tile), F32),
            pltpu.VMEM((tile, tile), F32),
            dma((n_load,)),
            dma((n_off,)),
            dma((n_off,)),
            dma((n_c,)),
            dma((n_c,)),
            dma((n_off,)),
            dma((n_off,)),
        ],
        compiler_params=pltpu.CompilerParams(
            collective_id=0, has_side_effects=True, vmem_limit_bytes=56 * 2**20
        ),
    )(*operands)

    return pl.pallas_call(
        back_kernel,
        out_shape=(
            jax.ShapeDtypeStruct((tile, tile), F32),
            jax.ShapeDtypeStruct((tile, tile), BF),
        ),
        in_specs=[in_vmem] * 5,
        out_specs=(in_hbm, in_hbm),
        scratch_shapes=[
            pltpu.VMEM((tile, tile), F32),
            pltpu.VMEM((tile, tile), BF),
            dma((2 * (tile // min(MARGIN, 128)),)),
        ],
        compiler_params=pltpu.CompilerParams(vmem_limit_bytes=16 * 2**20),
    )(*kept)


def solution(mesh):
    in_specs = (P("ty", "tx"), P("ty", "tx"), P("ty", "tx"), P("cond", None, None, None, None))
    out_specs = (P("ty", "tx"), P("ty", "tx"))
    return jax.shard_map(
        per_device, mesh=mesh, in_specs=in_specs, out_specs=out_specs, check_vma=False
    )
```

```python
import functools
import math

import jax
import jax.numpy as jnp
import numpy as np
from jax import lax
from jax.experimental import pallas as pl
from jax.experimental.pallas import tpu as pltpu
from jax.sharding import PartitionSpec as P

MARGIN = 128
STEEPNESS = 6.0
THRESHOLD = 0.25
STEP_SIZE = 4.0
LANES = 128
HALF = 16
SLOT = 2 * HALF
SLOTS = LANES // SLOT
WIDE = 64
MESH = pl.DeviceIdType.MESH
BF = jnp.bfloat16
F32 = jnp.float32


def halves(table):
    table = np.asarray(table, np.float32)
    high = table.astype(BF)
    return high, (table - high.astype(np.float32)).astype(BF)


def place(rows, cols, *pieces):
    out = np.zeros((rows, cols))
    for top, left, piece in pieces:
        out[top : top + piece.shape[0], left : left + piece.shape[1]] = piece
    return out


def trig(positions, top, period):
    turns = np.mod(np.outer(positions, np.arange(top + 1)), period).astype(np.float64)
    angle = turns * (2 * math.pi / period)
    return place(len(positions), SLOT, (0, 0, np.cos(angle)), (0, HALF, np.sin(angle)))


def make_tables(tile, margin, band):
    top = band // 2
    assert band % 2 == 0 and top < HALF and tile >= 2 * margin
    length = tile + 2 * margin
    grid = -(-(2 * band - 1) // 16) * 16
    assert grid <= WIDE
    shifted = []
    for step in (-1, 0, 1):
        spots = np.arange(tile) + margin - step * tile
        inside = ((spots >= 0) & (spots < length))[:, None]
        shifted.append(trig(spots, top, length) * inside)
    wave = np.concatenate(shifted, 1)
    fh, fl = halves(wave)
    pad = np.zeros((tile, LANES - 3 * SLOT), fh.dtype)
    fcol = np.concatenate([fh, pad, fl, pad], 1)
    frow = np.concatenate([fh.T, fl.T], 0)

    ec = trig(np.arange(grid), top, grid)
    bh, bl = halves(ec)
    norm = 1.0 / (length * length)
    sh, sl = halves(ec * norm)
    block = place(LANES, SLOTS * WIDE, *((SLOT * j, WIDE * j, ec.T) for j in range(SLOTS)))
    th, tl = halves(block)
    turn = (np.arange(tile) + margin)[:, None] / length - np.arange(grid)[None, :] / grid
    orders = np.arange(1, band)
    interp = (1 + 2 * np.cos(2 * math.pi * turn[:, :, None] * orders).sum(-1)) / grid
    ih, il = halves(interp)
    gap = np.zeros((tile, WIDE - grid), ih.dtype)
    wn = np.concatenate([ih, gap, ih, gap, il, gap, il, gap], 1)
    wt = np.concatenate([ih.T, il.T], 0)

    plus, minus = np.zeros((HALF, band)), np.zeros((HALF, band))
    for m in range(top):
        plus[m, top + m] = 1
    for m in range(1, top + 1):
        minus[m, top - m] = 1
    even, odd = plus + minus, plus - minus
    kl = np.concatenate([even, even, -odd, odd], 0)
    kr = np.stack([
        place(
            band, 2 * LANES,
            (0, SLOT * j, even.T), (0, SLOT * j + HALF, even.T),
            (0, LANES + SLOT * j, -odd.T), (0, LANES + SLOT * j + HALF, odd.T),
        )
        for j in range(SLOTS)
    ])
    front = dict(
        fcol=fcol, frow=frow, kr=kr.astype(BF), kl=kl.astype(BF),
        left=np.concatenate([sh, sh, sl], 1),
        th=th, tl=tl, wt=wt, wn=wn,
        tb=np.concatenate([th.T, tl.T], 1),
        lt=np.concatenate([bh.T, bh.T, bl.T], 1),
    )
    edge, mid = [0, SLOT], [SLOT, 2 * SLOT]
    rows = np.zeros((tile, 6 * SLOT), fh.dtype)
    for lo, hi, cut in ((0, margin, 0), (tile - margin, tile, SLOT)):
        pick = slice(cut, cut + 2 * SLOT)
        rows[lo:hi] = np.concatenate([fh[lo:hi, pick], fh[lo:hi, pick], fl[lo:hi, pick]], 1)
    lo, hi, pick = margin, tile - margin, slice(SLOT, 2 * SLOT)
    rows[lo:hi, : 3 * SLOT] = np.concatenate([fh[lo:hi, pick], fh[lo:hi, pick], fl[lo:hi, pick]], 1)
    back = dict(frow=frow, brow=rows)
    return front, back, grid


def split(x):
    high = x.astype(BF)
    return high, (x - high.astype(F32)).astype(BF)


def mm(a, b):
    return jnp.dot(a, b, preferred_element_type=F32)


def roll(x, shift):
    shift = shift % LANES
    return x if shift == 0 else pltpu.roll(x, shift, 1)


def by_slot(pieces):
    lane = lax.broadcasted_iota(jnp.int32, pieces[0].shape, 1)
    out = pieces[-1]
    for j in range(len(pieces) - 2, -1, -1):
        out = jnp.where(lane < (j + 1) * SLOT, pieces[j], out)
    return out


def swap(x):
    return jnp.concatenate([x[HALF:], x[:HALF]], 0)


def neighbours(ty, tx, n_ty, n_tx):
    here = (0, None, 0)
    if n_ty == 2:
        vert = [here, (1 - 2 * ty, None, 1)]
    else:
        vert = [here, (-1, ty > 0, 2), (1, ty < n_ty - 1, 1)][: 1 if n_ty == 1 else 3]
    side = [here, (-1, tx > 0, 2), (1, tx < n_tx - 1, 1)]
    spots = [(v, h) for v in range(len(vert)) for h in range(len(side))]

    def groups(mirror):
        out = {}
        for v, h in spots:
            keys = (vert[v][2], side[h][2]) if mirror else (v, h)
            key = (keys[0] if vert[v][1] is not None else 0, keys[1])
            out.setdefault(key, []).append((v, h))
        for (v, h), members in out.items():
            tests = [t for t in (vert[v][1], side[h][1]) if t is not None]
            ok = None if not tests else tests[0] if len(tests) == 1 else tests[0] & tests[1]
            yield ok, members

    return vert, side, spots, groups


def front_kernel(names, grid, n_k, *refs):
    n_tab = len(names)
    logits_hbm, target_hbm, weight_hbm, kern_hbm = refs[:4]
    tab_hbm = dict(zip(names, refs[4 : 4 + n_tab]))
    late_hbm = refs[4 + n_tab]
    out_ref, logits, fac, frow, late = refs[5 + n_tab : 10 + n_tab]
    rest = refs[10 + n_tab :]
    target, weight, kern = rest[:3]
    own = [n for n in names if n != "frow"]
    tab = dict(zip(own, rest[3 : 3 + len(own)]), frow=frow)
    (kq, send1, recv1, zs_own, recv2, level, signed,
     load_sem, s1, r1, s2, r2) = rest[3 + len(own) :]

    tile = logits.shape[0]
    band = kern.shape[-1]
    n_g = n_k // SLOTS
    length = tile + 2 * MARGIN
    norm = 1.0 / (length * length)
    chunk = min(tile, 256)
    parts = [slice(i, i + chunk) for i in range(0, tile, chunk)]
    n_ty, n_tx, n_c = lax.axis_size("ty"), lax.axis_size("tx"), lax.axis_size("cond")
    ty, tx, me = lax.axis_index("ty"), lax.axis_index("tx"), lax.axis_index("cond")

    jobs = [("fcol", tab_hbm["fcol"], tab["fcol"])]
    jobs += [(part.start, logits_hbm.at[part], logits.at[part]) for part in parts]
    jobs += [("frow", tab_hbm["frow"], frow), ("kern", kern_hbm, kern)]
    jobs += [(n, tab_hbm[n], tab[n]) for n in ("kr", "kl")]
    jobs += [("target", target_hbm, target), ("weight", weight_hbm, weight)]
    jobs += [(n, tab_hbm[n], tab[n]) for n in own if n not in ("fcol", "kr", "kl")]
    jobs += [("late", late_hbm, late)]
    loads = {}
    for i, (name, source, dest) in enumerate(jobs):
        loads[name] = pltpu.make_async_copy(source, dest, load_sem.at[i])
        loads[name].start()

    vert, side, spots, groups = neighbours(ty, tx, n_ty, n_tx)

    def target_of(spot, turn=0):
        v, h = spot
        where = {"ty": ty + vert[v][0], "tx": tx + side[h][0]}
        return dict(where, cond=lax.rem(me + turn, n_c)) if turn else where

    def each(mirror, turns, act):
        for ok, members in groups(mirror):
            jobs_here = [(m, t) for m in members for t in turns if m != (0, 0) or t]

            def run(jobs_here=jobs_here):
                for spot, turn in jobs_here:
                    act(spot, turn)

            if not jobs_here:
                continue
            if ok is None:
                run()
            else:
                pl.when(ok)(run)

    barrier = pltpu.get_barrier_semaphore()
    each(False, range(n_c), lambda spot, turn: pl.semaphore_signal(
        barrier, inc=1, device_id=target_of(spot, turn), device_id_type=MESH
    ))
    for ok, members in groups(True):
        if ok is None:
            continue

        @pl.when(jnp.logical_not(ok))
        def _():
            for spot in members:
                recv1[spots.index(spot)] = jnp.zeros(recv1.shape[1:], F32)
                for turn in range(n_c):
                    recv2[turn, spots.index(spot)] = jnp.zeros(recv2.shape[2:], F32)

    loads["fcol"].wait()
    share = None
    for i, part in enumerate(parts):
        loads[part.start].wait()
        mh, ml = split(0.5 + 0.5 * jnp.tanh(logits[part]))
        both = mm(mh, tab["fcol"][...])
        proj = both[:, :LANES] + both[:, LANES:] + mm(ml, tab["fcol"][:, :LANES])
        if i == 0:
            loads["frow"].wait()
        piece = mm(frow[:, part], jnp.concatenate(split(proj), 1))
        share = piece if share is None else share + piece
    n_f = 3 * SLOT
    share = share[:n_f, :LANES] + share[:n_f, LANES:] + share[n_f:, :LANES]
    strips = {0: share[SLOT : 2 * SLOT]}
    for v in range(1, len(vert)):
        above, below = share[:SLOT], share[2 * SLOT :]
        dr = vert[v][0]
        strips[v] = (above if dr < 0 else below) if isinstance(dr, int) else jnp.where(dr < 0, above, below)
    for i, (v, h) in enumerate(spots):
        send1[i] = by_slot(
            [roll(strips[v][8 * t : 8 * t + 8], SLOT * (t - side[h][0] - 1)) for t in range(SLOTS)]
        )

    peers = -1
    for ok, members in groups(True):
        peers = peers + n_c * len(members) * (1 if ok is None else ok.astype(jnp.int32))
    pl.semaphore_wait(barrier, peers)

    def first(spot, turn=0):
        i = spots.index(spot)
        return pltpu.make_async_remote_copy(
            src_ref=send1.at[i], dst_ref=recv1.at[i], send_sem=s1.at[i], recv_sem=r1.at[i],
            device_id=target_of(spot), device_id_type=MESH,
        )

    def second(spot, turn):
        i = spots.index(spot)
        return pltpu.make_async_remote_copy(
            src_ref=zs_own, dst_ref=recv2.at[turn, i], send_sem=s2.at[turn, i],
            recv_sem=r2.at[turn, i], device_id=target_of(spot, turn), device_id_type=MESH,
        )

    each(False, (0,), lambda spot, turn: first(spot).start())

    for name in ("kern", "kr", "kl"):
        loads[name].wait()
    turned = None
    for j in range(SLOTS):
        rows = jnp.concatenate(
            [kern[0, SLOTS * g + j, ri] for g in range(n_g) for ri in range(2)], 0
        )
        high, low = split(rows)
        piece = mm(high, tab["kr"][j]) + mm(low, tab["kr"][j])
        turned = piece if turned is None else turned + piece
    for e in range(2 * n_g):
        high, low = split(turned[e * band : (e + 1) * band])
        kq[:, 2 * LANES * e : 2 * LANES * (e + 1)] = mm(tab["kl"][...], high) + mm(tab["kl"][...], low)
    loads["target"].wait()
    loads["weight"].wait()

    def prepare(i, carry):
        part = pl.ds(pl.multiple_of(i * 32, 32), 32)
        vals = weight[part].astype(F32)
        level[part] = vals
        signed[part] = vals * (2.0 * target[part].astype(F32) - 1.0)
        mask = jnp.tanh(logits[part])
        fac[part] = (1.5 * STEP_SIZE * norm) * (mask * mask - 1.0)
        return carry

    lax.fori_loop(0, tile // 32, prepare, 0)
    for name in own:
        if name not in ("fcol", "kr", "kl"):
            loads[name].wait()
    loads["late"].wait()

    each(True, (0,), lambda spot, turn: first(spot).wait_recv())
    spec = send1[0]
    for i in range(1, len(spots)):
        spec = spec + recv1[i]

    turns = [roll(spec, SLOT * s) for s in range(SLOTS)]
    u = jnp.concatenate(
        [by_slot([turns[(j - t) % SLOTS] for j in range(SLOTS)]) for t in range(SLOTS)], 0
    )
    v = roll(u, HALF)
    us, vs = swap(u), swap(v)

    def quarter(e, row, col):
        left = 2 * LANES * e + LANES * col
        return kq[SLOT * row : SLOT * (row + 1), left : left + LANES]

    coef = []
    for g in range(n_g):
        r, i = 2 * g, 2 * g + 1
        coef.append(quarter(r, 0, 0) * u - quarter(r, 1, 1) * vs - quarter(i, 1, 0) * us - quarter(i, 0, 1) * v)
        coef.append(quarter(i, 0, 0) * u - quarter(i, 1, 1) * vs + quarter(r, 1, 0) * us + quarter(r, 0, 1) * v)
    n_e = 2 * n_g
    ah, al = split(jnp.concatenate(coef, 1))
    half = mm(tab["left"][...], jnp.concatenate([ah, al, ah], 0))
    hh, hl = split(jnp.concatenate([half[:, LANES * e : LANES * (e + 1)] for e in range(n_e)], 0))
    field = mm(hh, tab["th"][...]) + mm(hl, tab["th"][...]) + mm(hh, tab["tl"][...])
    coarse = jnp.zeros((grid, 2 * LANES), F32)
    for e in range(n_e):
        cut = field[grid * e : grid * (e + 1)]
        coarse = coarse + cut * cut
    coarse = coarse[:, :LANES] + coarse[:, LANES:]
    coarse = (0.5 * STEEPNESS) * (coarse + roll(coarse, WIDE) - THRESHOLD)
    ch, cl = split(coarse[:, :grid])
    wt = tab["wt"]
    uh, ul = split(mm(ch, wt[:grid]) + mm(cl, wt[:grid]) + mm(ch, wt[grid:]))
    gap = jnp.zeros((WIDE - grid, tile), BF)
    ustack = jnp.concatenate([uh, gap, ul, gap, uh, gap, gap, gap, gap, gap], 0)[: 4 * WIDE]

    gsum = None
    for part in [slice(0, tile)]:
        th = jnp.tanh(mm(tab["wn"][part], ustack))
        gain = (level[part] * th - signed[part]) * (1.0 - th * th)
        gh, gl = split(gain)
        wide = mm(gh, tab["wn"][...])
        y = wide[:, :LANES] + wide[:, LANES:] + mm(gl, tab["wn"][:, :LANES])
        piece = mm(wt[:, part], jnp.concatenate(split(y), 1))
        gsum = piece if gsum is None else gsum + piece
    gcoarse = gsum[:grid, :LANES] + gsum[:grid, LANES:] + gsum[grid:, :LANES]

    gpair = jnp.concatenate([gcoarse, gcoarse], 1)
    dh, dl = split(jnp.concatenate([gpair * field[grid * e : grid * (e + 1)] for e in range(n_e)], 0))
    wide = mm(dh, tab["tb"][...])
    down = wide[:, :LANES] + wide[:, LANES:] + mm(dl, tab["tb"][:, :LANES])
    eh, el = split(jnp.concatenate([down[grid * e : grid * (e + 1)] for e in range(n_e)], 1))
    d = mm(tab["lt"][...], jnp.concatenate([eh, el, eh], 0))
    du = jnp.zeros((SLOT, LANES), F32)
    dus, dv, dvs = du, du, du
    for g in range(n_g):
        r, i = 2 * g, 2 * g + 1
        dr_, di_ = d[:, LANES * r : LANES * (r + 1)], d[:, LANES * i : LANES * (i + 1)]
        du = du + quarter(r, 0, 0) * dr_ + quarter(i, 0, 0) * di_
        dus = dus + quarter(r, 1, 0) * di_ - quarter(i, 1, 0) * dr_
        dv = dv + quarter(r, 0, 1) * di_ - quarter(i, 0, 1) * dr_
        dvs = dvs - quarter(r, 1, 1) * dr_ - quarter(i, 1, 1) * di_
    dx = du + swap(dus) + roll(dv + swap(dvs), HALF)
    x = [dx[8 * t : 8 * t + 8] for t in range(SLOTS)]
    lane = lax.broadcasted_iota(jnp.int32, (8, LANES), 1)
    even, low = (lane // SLOT) % 2 == 0, lane < 2 * SLOT
    pair = [
        jnp.where(even, a, b) + jnp.where(
            even, roll(jnp.where(even, b, a), -SLOT), roll(jnp.where(even, b, a), SLOT)
        )
        for a, b in ((x[0], x[1]), (x[2], x[3]))
    ]
    zs_own[...] = jnp.where(low, pair[0], pair[1]) + roll(jnp.where(low, pair[1], pair[0]), 2 * SLOT)

    each(False, tuple(range(n_c))[::-1], lambda spot, turn: second(spot, turn).start())
    recv2[0, 0] = zs_own[...]
    each(True, range(n_c), lambda spot, turn: second(spot, turn).wait_recv())
    blocks = {}
    for i, (v, h) in enumerate(spots):
        total = recv2[0, i]
        for turn in range(1, n_c):
            total = total + recv2[turn, i]
        blocks[v, h] = total
    bands = []
    for v in range(len(vert)):
        line = [blocks[v, h] for h in (2, 0, 1)]
        bands.append(jnp.concatenate(
            [by_slot([roll(b, SLOT * (i - t)) for i, b in enumerate(line)]) for t in range(SLOTS)], 0
        ))
    none = jnp.zeros((SLOT, LANES), F32)
    if len(vert) == 1:
        above = below = none
    elif len(vert) == 2:
        above = jnp.where(vert[1][0] < 0, bands[1], none)
        below = jnp.where(vert[1][0] < 0, none, bands[1])
    else:
        above, below = bands[2], bands[1]
    out_ref[:SLOT] = above
    out_ref[SLOT : 2 * SLOT] = bands[0]
    out_ref[2 * SLOT :] = below

    each(False, (0,), lambda spot, turn: first(spot).wait_send())
    each(False, range(n_c), lambda spot, turn: second(spot, turn).wait_send())


def back_kernel(z_ref, logits, fac, frow, brow, new_hbm, next_hbm, new, nxt, sem):
    tile = logits.shape[1]
    n_f = 3 * SLOT
    zh, zl = split(z_ref[:, :n_f])
    w = mm(zh, frow[:n_f]) + mm(zl, frow[:n_f]) + mm(zh, frow[n_f:])
    wh, wl = split(w)

    chunk = min(MARGIN, 128)
    copies = []
    for i in range(tile // chunk):
        lo, hi = i * chunk, (i + 1) * chunk
        part = slice(lo, hi)
        first = 0 if lo < MARGIN else SLOT
        last = 3 * SLOT if hi > tile - MARGIN else 2 * SLOT
        pick = slice(first, last)
        stack = jnp.concatenate([wh[pick], wl[pick], wh[pick]], 0)
        grad = mm(brow[part, : 3 * (last - first)], stack)
        value = logits[part] + fac[part] * grad
        new[part] = value
        nxt[part] = (0.5 + 0.5 * jnp.tanh(value)).astype(BF)
        for j, (buf, out) in enumerate(((new, new_hbm), (nxt, next_hbm))):
            copy = pltpu.make_async_copy(buf.at[part], out.at[part], sem.at[2 * i + j])
            copy.start()
            copies.append(copy)
    for copy in copies:
        copy.wait()


def per_device(mask_logits, target_layout, density_weights, socs_kernels):
    tile = mask_logits.shape[0]
    band = socs_kernels.shape[-1]
    n_k = socs_kernels.shape[1]
    assert n_k % SLOTS == 0
    n_c, n_ty = lax.axis_size("cond"), lax.axis_size("ty")
    front, back, grid = make_tables(tile, MARGIN, band)
    names = list(front)
    arrays = [mask_logits, target_layout, density_weights, socs_kernels]
    tables = {n: jnp.asarray(front[n]) for n in names}
    late = jnp.asarray(back["brow"])
    in_vmem = pl.BlockSpec(memory_space=pltpu.VMEM)
    in_hbm = pl.BlockSpec(memory_space=pl.ANY)
    vmem = lambda a: pltpu.VMEM(a.shape, a.dtype)
    dma = pltpu.SemaphoreType.DMA
    n_off = 3 * min(n_ty, 3)
    held = (8, LANES)
    n_load = len(names) + 5 + tile // min(tile, 256)
    operands = arrays + [tables[n] for n in names] + [late]
    kept = pl.pallas_call(
        functools.partial(front_kernel, names, grid, n_k),
        out_shape=[
            pltpu.VMEM((3 * SLOT, LANES), F32), pltpu.VMEM((tile, tile), F32),
            pltpu.VMEM((tile, tile), F32), vmem(tables["frow"]), vmem(late),
        ],
        in_specs=[in_hbm] * len(operands),
        out_specs=[in_vmem] * 5,
        scratch_shapes=[vmem(a) for a in arrays[1:]]
        + [vmem(tables[n]) for n in names if n != "frow"]
        + [
            pltpu.VMEM((2 * SLOT, 2 * LANES * 2 * n_k // SLOTS), F32),
            pltpu.VMEM((n_off, *held), F32),
            pltpu.VMEM((n_off, *held), F32),
            pltpu.VMEM(held, F32),
            pltpu.VMEM((n_c, n_off, *held), F32),
            pltpu.VMEM((tile, tile), F32),
            pltpu.VMEM((tile, tile), F32),
            dma((n_load,)),
            dma((n_off,)),
            dma((n_off,)),
            dma((n_c, n_off)),
            dma((n_c, n_off)),
        ],
        compiler_params=pltpu.CompilerParams(
            collective_id=0, has_side_effects=True, vmem_limit_bytes=56 * 2**20
        ),
    )(*operands)

    return pl.pallas_call(
        back_kernel,
        out_shape=(
            jax.ShapeDtypeStruct((tile, tile), F32),
            jax.ShapeDtypeStruct((tile, tile), BF),
        ),
        in_specs=[in_vmem] * 5,
        out_specs=(in_hbm, in_hbm),
        scratch_shapes=[
            pltpu.VMEM((tile, tile), F32),
            pltpu.VMEM((tile, tile), BF),
            dma((2 * (tile // min(MARGIN, 128)),)),
        ],
        compiler_params=pltpu.CompilerParams(vmem_limit_bytes=16 * 2**20),
    )(*kept)


def solution(mesh):
    in_specs = (P("ty", "tx"), P("ty", "tx"), P("ty", "tx"), P("cond", None, None, None, None))
    out_specs = (P("ty", "tx"), P("ty", "tx"))
    return jax.shard_map(
        per_device, mesh=mesh, in_specs=in_specs, out_specs=out_specs, check_vma=False
    )
```

```python
import functools
import math

import jax
import jax.numpy as jnp
import numpy as np
from jax import lax
from jax.experimental import pallas as pl
from jax.experimental.pallas import tpu as pltpu
from jax.sharding import PartitionSpec as P

MARGIN = 128
STEEPNESS = 6.0
THRESHOLD = 0.25
STEP_SIZE = 4.0
LANES = 128
HALF = 16
USED = 7
SLOT = 2 * HALF
SLOTS = LANES // SLOT
WIDE = 64
MESH = pl.DeviceIdType.MESH
BF = jnp.bfloat16
F32 = jnp.float32


def halves(table):
    table = np.asarray(table, np.float32)
    high = table.astype(BF)
    return high, (table - high.astype(np.float32)).astype(BF)


def place(rows, cols, *pieces):
    out = np.zeros((rows, cols))
    for top, left, piece in pieces:
        out[top : top + piece.shape[0], left : left + piece.shape[1]] = piece
    return out


def spread(order):
    return order + order // USED


def trig(positions, top, period):
    turns = np.mod(np.outer(positions, np.arange(top + 1)), period).astype(np.float64)
    angle = turns * (2 * math.pi / period)
    out = np.zeros((len(positions), SLOT))
    out[:, spread(np.arange(top + 1))] = np.cos(angle)
    out[:, HALF + spread(np.arange(top + 1))] = np.sin(angle)
    return out


def make_tables(tile, margin, band):
    top = band // 2
    assert band % 2 == 0 and spread(top) < HALF and tile >= 2 * margin
    length = tile + 2 * margin
    grid = -(-(2 * band - 1) // 16) * 16
    assert grid <= WIDE
    shifted = []
    for step in (-1, 0, 1):
        spots = np.arange(tile) + margin - step * tile
        inside = ((spots >= 0) & (spots < length))[:, None]
        shifted.append(trig(spots, top, length) * inside)
    wave = np.concatenate(shifted, 1)
    fh, fl = halves(wave)
    pad = np.zeros((tile, LANES - 3 * SLOT), fh.dtype)
    fcol = np.concatenate([fh, pad, fl, pad], 1)
    frow = np.concatenate([fh.T, fl.T], 0)

    ec = trig(np.arange(grid), top, grid)
    bh, bl = halves(ec)
    norm = 1.0 / (length * length)
    sh, sl = halves(ec * norm)
    block = place(LANES, SLOTS * WIDE, *((SLOT * j, WIDE * j, ec.T) for j in range(SLOTS)))
    th, tl = halves(block)
    turn = (np.arange(tile) + margin)[:, None] / length - np.arange(grid)[None, :] / grid
    orders = np.arange(1, band)
    interp = (1 + 2 * np.cos(2 * math.pi * turn[:, :, None] * orders).sum(-1)) / grid
    ih, il = halves(interp)
    gap = np.zeros((tile, WIDE - grid), ih.dtype)
    wn = np.concatenate([ih, gap, ih, gap, il, gap, il, gap], 1)
    wt = np.concatenate([ih.T, il.T], 0)

    plus, minus = np.zeros((HALF, band)), np.zeros((HALF, band))
    for m in range(top):
        plus[spread(m), top + m] = 1
    for m in range(1, top + 1):
        minus[spread(m), top - m] = 1
    even, odd = plus + minus, plus - minus
    kl = np.concatenate([even, even, -odd, odd], 0)
    kr = np.stack([
        place(
            band, 2 * LANES,
            (0, SLOT * j, even.T), (0, SLOT * j + HALF, even.T),
            (0, LANES + SLOT * j, -odd.T), (0, LANES + SLOT * j + HALF, odd.T),
        )
        for j in range(SLOTS)
    ])
    front = dict(
        fcol=fcol, frow=frow, kr=kr.astype(BF), kl=kl.astype(BF),
        left=np.concatenate([sh, sh, sl], 1),
        th=th, tl=tl, wt=wt, wn=wn,
        tb=np.concatenate([th.T, tl.T], 1),
        lt=np.concatenate([bh.T, bh.T, bl.T], 1),
    )
    edge, mid = [0, SLOT], [SLOT, 2 * SLOT]
    rows = np.zeros((tile, 6 * SLOT), fh.dtype)
    for lo, hi, cut in ((0, margin, 0), (tile - margin, tile, SLOT)):
        pick = slice(cut, cut + 2 * SLOT)
        rows[lo:hi] = np.concatenate([fh[lo:hi, pick], fh[lo:hi, pick], fl[lo:hi, pick]], 1)
    lo, hi, pick = margin, tile - margin, slice(SLOT, 2 * SLOT)
    rows[lo:hi, : 3 * SLOT] = np.concatenate([fh[lo:hi, pick], fh[lo:hi, pick], fl[lo:hi, pick]], 1)
    back = dict(frow=frow, brow=rows)
    return front, back, grid


def split(x):
    high = x.astype(BF)
    return high, (x - high.astype(F32)).astype(BF)


def mm(a, b):
    return jnp.dot(a, b, preferred_element_type=F32)


def roll(x, shift):
    shift = shift % LANES
    return x if shift == 0 else pltpu.roll(x, shift, 1)


def by_slot(pieces):
    lane = lax.broadcasted_iota(jnp.int32, pieces[0].shape, 1)
    out = pieces[-1]
    for j in range(len(pieces) - 2, -1, -1):
        out = jnp.where(lane < (j + 1) * SLOT, pieces[j], out)
    return out


def swap(x):
    return jnp.concatenate([x[HALF:], x[:HALF]], 0)


def neighbours(ty, tx, n_ty, n_tx):
    here = (0, None, 0)
    if n_ty == 2:
        vert = [here, (1 - 2 * ty, None, 1)]
    else:
        vert = [here, (-1, ty > 0, 2), (1, ty < n_ty - 1, 1)][: 1 if n_ty == 1 else 3]
    side = [here, (-1, tx > 0, 2), (1, tx < n_tx - 1, 1)]
    spots = [(v, h) for v in range(len(vert)) for h in range(len(side))]

    def groups(mirror):
        out = {}
        for v, h in spots:
            keys = (vert[v][2], side[h][2]) if mirror else (v, h)
            key = (keys[0] if vert[v][1] is not None else 0, keys[1])
            out.setdefault(key, []).append((v, h))
        for (v, h), members in out.items():
            tests = [t for t in (vert[v][1], side[h][1]) if t is not None]
            ok = None if not tests else tests[0] if len(tests) == 1 else tests[0] & tests[1]
            yield ok, members

    return vert, side, spots, groups


def front_kernel(names, grid, n_k, *refs):
    n_tab = len(names)
    logits_hbm, target_hbm, weight_hbm, kern_hbm = refs[:4]
    tab_hbm = dict(zip(names, refs[4 : 4 + n_tab]))
    late_hbm = refs[4 + n_tab]
    out_ref, logits, fac, frow, late = refs[5 + n_tab : 10 + n_tab]
    rest = refs[10 + n_tab :]
    target, weight, kern = rest[:3]
    own = [n for n in names if n != "frow"]
    tab = dict(zip(own, rest[3 : 3 + len(own)]), frow=frow)
    (kq, send1, recv1, zs_own, recv2, level, signed,
     load_sem, s1, r1, s2, r2) = rest[3 + len(own) :]

    tile = logits.shape[0]
    band = kern.shape[-1]
    n_g = n_k // SLOTS
    length = tile + 2 * MARGIN
    norm = 1.0 / (length * length)
    chunk = min(tile, 512)
    parts = [slice(i, i + chunk) for i in range(0, tile, chunk)]
    n_ty, n_tx, n_c = lax.axis_size("ty"), lax.axis_size("tx"), lax.axis_size("cond")
    ty, tx, me = lax.axis_index("ty"), lax.axis_index("tx"), lax.axis_index("cond")

    jobs = [("fcol", tab_hbm["fcol"], tab["fcol"])]
    jobs += [(part.start, logits_hbm.at[part], logits.at[part]) for part in parts]
    jobs += [("frow", tab_hbm["frow"], frow), ("kern", kern_hbm, kern)]
    jobs += [(n, tab_hbm[n], tab[n]) for n in ("kr", "kl")]
    jobs += [("target", target_hbm, target), ("weight", weight_hbm, weight)]
    jobs += [(n, tab_hbm[n], tab[n]) for n in own if n not in ("fcol", "kr", "kl")]
    jobs += [("late", late_hbm, late)]
    loads = {}
    for i, (name, source, dest) in enumerate(jobs):
        loads[name] = pltpu.make_async_copy(source, dest, load_sem.at[i])
        loads[name].start()

    vert, side, spots, groups = neighbours(ty, tx, n_ty, n_tx)

    def target_of(spot, turn=0):
        v, h = spot
        where = {"ty": ty + vert[v][0], "tx": tx + side[h][0]}
        away = not isinstance(turn, int) or turn
        return dict(where, cond=lax.rem(me + turn, n_c)) if away else where

    def each(mirror, turns, act):
        for ok, members in groups(mirror):
            jobs_here = [(m, t) for m in members for t in turns if m != (0, 0) or not isinstance(t, int) or t]

            def run(jobs_here=jobs_here):
                for spot, turn in jobs_here:
                    act(spot, turn)

            if not jobs_here:
                continue
            if ok is None:
                run()
            else:
                pl.when(ok)(run)

    barrier = pltpu.get_barrier_semaphore()
    each(False, range(n_c), lambda spot, turn: pl.semaphore_signal(
        barrier, inc=1, device_id=target_of(spot, turn), device_id_type=MESH
    ))
    for ok, members in groups(True):
        if ok is None:
            continue

        @pl.when(jnp.logical_not(ok))
        def _():
            for spot in members:
                recv1[spots.index(spot)] = jnp.zeros(recv1.shape[1:], F32)
                for turn in range(n_c):
                    recv2[turn, spots.index(spot)] = jnp.zeros(recv2.shape[2:], F32)

    loads["fcol"].wait()
    share = None
    for i, part in enumerate(parts):
        loads[part.start].wait()
        mh, ml = split(0.5 + 0.5 * jnp.tanh(logits[part]))
        both = mm(mh, tab["fcol"][...])
        proj = both[:, :LANES] + both[:, LANES:] + mm(ml, tab["fcol"][:, :LANES])
        if i == 0:
            loads["frow"].wait()
        piece = mm(frow[:, part], jnp.concatenate(split(proj), 1))
        share = piece if share is None else share + piece
    n_f = 3 * SLOT
    share = share[:n_f, :LANES] + share[:n_f, LANES:] + share[n_f:, :LANES]
    strips = {0: share[SLOT : 2 * SLOT]}
    for v in range(1, len(vert)):
        above, below = share[:SLOT], share[2 * SLOT :]
        dr = vert[v][0]
        strips[v] = (above if dr < 0 else below) if isinstance(dr, int) else jnp.where(dr < 0, above, below)
    for i, (v, h) in enumerate(spots):
        send1[i] = by_slot(
            [roll(strips[v][8 * t : 8 * t + 8], SLOT * (t - side[h][0] - 1)) for t in range(SLOTS)]
        )[:USED]

    peers = -1
    for ok, members in groups(True):
        peers = peers + n_c * len(members) * (1 if ok is None else ok.astype(jnp.int32))
    pl.semaphore_wait(barrier, peers)

    def first(spot, turn=0):
        i = spots.index(spot)
        return pltpu.make_async_remote_copy(
            src_ref=send1.at[i], dst_ref=recv1.at[i], send_sem=s1.at[i], recv_sem=r1.at[i],
            device_id=target_of(spot), device_id_type=MESH,
        )

    def second(spot, turn):
        i = spots.index(spot)
        return pltpu.make_async_remote_copy(
            src_ref=zs_own, dst_ref=recv2.at[turn, i], send_sem=s2.at[turn, i],
            recv_sem=r2.at[turn, i], device_id=target_of(spot, turn), device_id_type=MESH,
        )

    each(False, (0,), lambda spot, turn: first(spot).start())

    for name in ("kern", "kr", "kl"):
        loads[name].wait()
    turned = None
    for j in range(SLOTS):
        rows = jnp.concatenate(
            [kern[0, SLOTS * g + j, ri] for g in range(n_g) for ri in range(2)], 0
        )
        high, low = split(rows)
        piece = mm(high, tab["kr"][j]) + mm(low, tab["kr"][j])
        turned = piece if turned is None else turned + piece
    for e in range(2 * n_g):
        high, low = split(turned[e * band : (e + 1) * band])
        kq[:, 2 * LANES * e : 2 * LANES * (e + 1)] = mm(tab["kl"][...], high) + mm(tab["kl"][...], low)
    loads["target"].wait()
    loads["weight"].wait()

    def prepare(i, carry):
        part = pl.ds(pl.multiple_of(i * 32, 32), 32)
        vals = weight[part].astype(F32)
        level[part] = vals
        signed[part] = vals * (2.0 * target[part].astype(F32) - 1.0)
        mask = jnp.tanh(logits[part])
        fac[part] = (1.5 * STEP_SIZE * norm) * (mask * mask - 1.0)
        return carry

    lax.fori_loop(0, tile // 32, prepare, 0)
    for name in own:
        if name not in ("fcol", "kr", "kl"):
            loads[name].wait()
    loads["late"].wait()

    each(True, (0,), lambda spot, turn: first(spot).wait_recv())
    spec = send1[0]
    for i in range(1, len(spots)):
        spec = spec + recv1[i]
    rest8 = jnp.zeros((8 - USED, LANES), F32)
    spec = jnp.concatenate([spec, rest8], 0)

    turns = [roll(spec, SLOT * s) for s in range(SLOTS)]
    u = jnp.concatenate(
        [by_slot([turns[(j - t) % SLOTS] for j in range(SLOTS)]) for t in range(SLOTS)], 0
    )
    v = roll(u, HALF)
    us, vs = swap(u), swap(v)

    def quarter(e, row, col):
        left = 2 * LANES * e + LANES * col
        return kq[SLOT * row : SLOT * (row + 1), left : left + LANES]

    coef = []
    for g in range(n_g):
        r, i = 2 * g, 2 * g + 1
        coef.append(quarter(r, 0, 0) * u - quarter(r, 1, 1) * vs - quarter(i, 1, 0) * us - quarter(i, 0, 1) * v)
        coef.append(quarter(i, 0, 0) * u - quarter(i, 1, 1) * vs + quarter(r, 1, 0) * us + quarter(r, 0, 1) * v)
    n_e = 2 * n_g
    ah, al = split(jnp.concatenate(coef, 1))
    half = mm(tab["left"][...], jnp.concatenate([ah, al, ah], 0))
    hh, hl = split(jnp.concatenate([half[:, LANES * e : LANES * (e + 1)] for e in range(n_e)], 0))
    field = mm(hh, tab["th"][...]) + mm(hl, tab["th"][...]) + mm(hh, tab["tl"][...])
    coarse = jnp.zeros((grid, 2 * LANES), F32)
    for e in range(n_e):
        cut = field[grid * e : grid * (e + 1)]
        coarse = coarse + cut * cut
    coarse = coarse[:, :LANES] + coarse[:, LANES:]
    coarse = (0.5 * STEEPNESS) * (coarse + roll(coarse, WIDE) - THRESHOLD)
    ch, cl = split(coarse[:, :grid])
    wt = tab["wt"]
    uh, ul = split(mm(ch, wt[:grid]) + mm(cl, wt[:grid]) + mm(ch, wt[grid:]))
    gap = jnp.zeros((WIDE - grid, tile), BF)
    ustack = jnp.concatenate([uh, gap, ul, gap, uh, gap, gap, gap, gap, gap], 0)[: 4 * WIDE]

    gsum = None
    for part in [slice(0, tile)]:
        th = jnp.tanh(mm(tab["wn"][part], ustack))
        gain = (level[part] * th - signed[part]) * (1.0 - th * th)
        gh, gl = split(gain)
        wide = mm(gh, tab["wn"][...])
        y = wide[:, :LANES] + wide[:, LANES:] + mm(gl, tab["wn"][:, :LANES])
        piece = mm(wt[:, part], jnp.concatenate(split(y), 1))
        gsum = piece if gsum is None else gsum + piece
    gcoarse = gsum[:grid, :LANES] + gsum[:grid, LANES:] + gsum[grid:, :LANES]

    gpair = jnp.concatenate([gcoarse, gcoarse], 1)
    dh, dl = split(jnp.concatenate([gpair * field[grid * e : grid * (e + 1)] for e in range(n_e)], 0))
    wide = mm(dh, tab["tb"][...])
    down = wide[:, :LANES] + wide[:, LANES:] + mm(dl, tab["tb"][:, :LANES])
    eh, el = split(jnp.concatenate([down[grid * e : grid * (e + 1)] for e in range(n_e)], 1))
    d = mm(tab["lt"][...], jnp.concatenate([eh, el, eh], 0))
    du = jnp.zeros((SLOT, LANES), F32)
    dus, dv, dvs = du, du, du
    for g in range(n_g):
        r, i = 2 * g, 2 * g + 1
        dr_, di_ = d[:, LANES * r : LANES * (r + 1)], d[:, LANES * i : LANES * (i + 1)]
        du = du + quarter(r, 0, 0) * dr_ + quarter(i, 0, 0) * di_
        dus = dus + quarter(r, 1, 0) * di_ - quarter(i, 1, 0) * dr_
        dv = dv + quarter(r, 0, 1) * di_ - quarter(i, 0, 1) * dr_
        dvs = dvs - quarter(r, 1, 1) * dr_ - quarter(i, 1, 1) * di_
    dx = du + swap(dus) + roll(dv + swap(dvs), HALF)
    x = [dx[8 * t : 8 * t + 8] for t in range(SLOTS)]
    lane = lax.broadcasted_iota(jnp.int32, (8, LANES), 1)
    even, low = (lane // SLOT) % 2 == 0, lane < 2 * SLOT
    pair = [
        jnp.where(even, a, b) + jnp.where(
            even, roll(jnp.where(even, b, a), -SLOT), roll(jnp.where(even, b, a), SLOT)
        )
        for a, b in ((x[0], x[1]), (x[2], x[3]))
    ]
    zs = jnp.where(low, pair[0], pair[1]) + roll(jnp.where(low, pair[1], pair[0]), 2 * SLOT)
    zs_own[...] = zs[:USED]

    high = (2 * me >= n_c).astype(jnp.int32)
    for k in range(n_c - 1):
        up = k + (k >= me).astype(jnp.int32)
        down = n_c - 1 - k - (n_c - 1 - k <= me).astype(jnp.int32)
        goal = high * up + (1 - high) * down
        turn = lax.rem(goal - me + n_c, n_c)
        each(False, (turn,), lambda spot, turn: second(spot, turn).start())
    each(False, (0,), lambda spot, turn: second(spot, turn).start())
    recv2[0, 0] = zs_own[...]
    each(True, range(n_c), lambda spot, turn: second(spot, turn).wait_recv())
    blocks = {}
    for i, (v, h) in enumerate(spots):
        total = recv2[0, i]
        for turn in range(1, n_c):
            total = total + recv2[turn, i]
        blocks[v, h] = jnp.concatenate([total, rest8], 0)
    bands = []
    for v in range(len(vert)):
        line = [blocks[v, h] for h in (2, 0, 1)]
        bands.append(jnp.concatenate(
            [by_slot([roll(b, SLOT * (i - t)) for i, b in enumerate(line)]) for t in range(SLOTS)], 0
        ))
    none = jnp.zeros((SLOT, LANES), F32)
    if len(vert) == 1:
        above = below = none
    elif len(vert) == 2:
        above = jnp.where(vert[1][0] < 0, bands[1], none)
        below = jnp.where(vert[1][0] < 0, none, bands[1])
    else:
        above, below = bands[2], bands[1]
    out_ref[:SLOT] = above
    out_ref[SLOT : 2 * SLOT] = bands[0]
    out_ref[2 * SLOT :] = below

    each(False, (0,), lambda spot, turn: first(spot).wait_send())
    each(False, range(n_c), lambda spot, turn: second(spot, turn).wait_send())


def back_kernel(z_ref, logits, fac, frow, brow, new_hbm, next_hbm, new, nxt, sem):
    tile = logits.shape[1]
    n_f = 3 * SLOT
    zh, zl = split(z_ref[:, :n_f])
    w = mm(zh, frow[:n_f]) + mm(zl, frow[:n_f]) + mm(zh, frow[n_f:])
    wh, wl = split(w)

    chunk = min(MARGIN, 128)
    copies = []
    for i in range(tile // chunk):
        lo, hi = i * chunk, (i + 1) * chunk
        part = slice(lo, hi)
        first = 0 if lo < MARGIN else SLOT
        last = 3 * SLOT if hi > tile - MARGIN else 2 * SLOT
        pick = slice(first, last)
        stack = jnp.concatenate([wh[pick], wl[pick], wh[pick]], 0)
        grad = mm(brow[part, : 3 * (last - first)], stack)
        value = logits[part] + fac[part] * grad
        new[part] = value
        nxt[part] = (0.5 + 0.5 * jnp.tanh(value)).astype(BF)
        for j, (buf, out) in enumerate(((new, new_hbm), (nxt, next_hbm))):
            copy = pltpu.make_async_copy(buf.at[part], out.at[part], sem.at[2 * i + j])
            copy.start()
            copies.append(copy)
    for copy in copies:
        copy.wait()


def per_device(mask_logits, target_layout, density_weights, socs_kernels):
    tile = mask_logits.shape[0]
    band = socs_kernels.shape[-1]
    n_k = socs_kernels.shape[1]
    assert n_k % SLOTS == 0
    n_c, n_ty = lax.axis_size("cond"), lax.axis_size("ty")
    front, back, grid = make_tables(tile, MARGIN, band)
    names = list(front)
    arrays = [mask_logits, target_layout, density_weights, socs_kernels]
    tables = {n: jnp.asarray(front[n]) for n in names}
    late = jnp.asarray(back["brow"])
    in_vmem = pl.BlockSpec(memory_space=pltpu.VMEM)
    in_hbm = pl.BlockSpec(memory_space=pl.ANY)
    vmem = lambda a: pltpu.VMEM(a.shape, a.dtype)
    dma = pltpu.SemaphoreType.DMA
    n_off = 3 * min(n_ty, 3)
    held = (USED, LANES)
    n_load = len(names) + 5 + tile // min(tile, 512)
    operands = arrays + [tables[n] for n in names] + [late]
    kept = pl.pallas_call(
        functools.partial(front_kernel, names, grid, n_k),
        out_shape=[
            pltpu.VMEM((3 * SLOT, LANES), F32), pltpu.VMEM((tile, tile), F32),
            pltpu.VMEM((tile, tile), F32), vmem(tables["frow"]), vmem(late),
        ],
        in_specs=[in_hbm] * len(operands),
        out_specs=[in_vmem] * 5,
        scratch_shapes=[vmem(a) for a in arrays[1:]]
        + [vmem(tables[n]) for n in names if n != "frow"]
        + [
            pltpu.VMEM((2 * SLOT, 2 * LANES * 2 * n_k // SLOTS), F32),
            pltpu.VMEM((n_off, *held), F32),
            pltpu.VMEM((n_off, *held), F32),
            pltpu.VMEM(held, F32),
            pltpu.VMEM((n_c, n_off, *held), F32),
            pltpu.VMEM((tile, tile), F32),
            pltpu.VMEM((tile, tile), F32),
            dma((n_load,)),
            dma((n_off,)),
            dma((n_off,)),
            dma((n_c, n_off)),
            dma((n_c, n_off)),
        ],
        compiler_params=pltpu.CompilerParams(
            collective_id=0, has_side_effects=True, vmem_limit_bytes=56 * 2**20
        ),
    )(*operands)

    return pl.pallas_call(
        back_kernel,
        out_shape=(
            jax.ShapeDtypeStruct((tile, tile), F32),
            jax.ShapeDtypeStruct((tile, tile), BF),
        ),
        in_specs=[in_vmem] * 5,
        out_specs=(in_hbm, in_hbm),
        scratch_shapes=[
            pltpu.VMEM((tile, tile), F32),
            pltpu.VMEM((tile, tile), BF),
            dma((2 * (tile // min(MARGIN, 128)),)),
        ],
        compiler_params=pltpu.CompilerParams(vmem_limit_bytes=16 * 2**20),
    )(*kept)


def solution(mesh):
    in_specs = (P("ty", "tx"), P("ty", "tx"), P("ty", "tx"), P("cond", None, None, None, None))
    out_specs = (P("ty", "tx"), P("ty", "tx"))
    return jax.shard_map(
        per_device, mesh=mesh, in_specs=in_specs, out_specs=out_specs, check_vma=False
    )
```

```python
import functools
import math

import jax
import jax.numpy as jnp
import numpy as np
from jax import lax
from jax.experimental import pallas as pl
from jax.experimental.pallas import tpu as pltpu
from jax.sharding import PartitionSpec as P

MARGIN = 128
STEEPNESS = 6.0
THRESHOLD = 0.25
STEP_SIZE = 4.0
LANES = 128
HALF = 16
USED = 7
SLOT = 2 * HALF
SLOTS = LANES // SLOT
WIDE = 64
MESH = pl.DeviceIdType.MESH
BF = jnp.bfloat16
F32 = jnp.float32


def halves(table):
    table = np.asarray(table, np.float32)
    high = table.astype(BF)
    return high, (table - high.astype(np.float32)).astype(BF)


def place(rows, cols, *pieces):
    out = np.zeros((rows, cols))
    for top, left, piece in pieces:
        out[top : top + piece.shape[0], left : left + piece.shape[1]] = piece
    return out


def spread(order):
    return order + order // USED


def trig(positions, top, period):
    turns = np.mod(np.outer(positions, np.arange(top + 1)), period).astype(np.float64)
    angle = turns * (2 * math.pi / period)
    out = np.zeros((len(positions), SLOT))
    out[:, spread(np.arange(top + 1))] = np.cos(angle)
    out[:, HALF + spread(np.arange(top + 1))] = np.sin(angle)
    return out


def make_tables(tile, margin, band):
    top = band // 2
    assert band % 2 == 0 and spread(top) < HALF and tile >= 2 * margin
    length = tile + 2 * margin
    grid = -(-(2 * band - 1) // 16) * 16
    assert grid <= WIDE
    shifted = []
    for step in (-1, 0, 1):
        spots = np.arange(tile) + margin - step * tile
        inside = ((spots >= 0) & (spots < length))[:, None]
        shifted.append(trig(spots, top, length) * inside)
    wave = np.concatenate(shifted, 1)
    fh, fl = halves(wave)
    pad = np.zeros((tile, LANES - 3 * SLOT), fh.dtype)
    fcol = np.concatenate([fh, pad, fl, pad], 1)
    frow = np.concatenate([fh.T, fl.T], 0)

    ec = trig(np.arange(grid), top, grid)
    bh, bl = halves(ec)
    norm = 1.0 / (length * length)
    sh, sl = halves(ec * norm)
    block = place(LANES, SLOTS * WIDE, *((SLOT * j, WIDE * j, ec.T) for j in range(SLOTS)))
    th, tl = halves(block)
    turn = (np.arange(tile) + margin)[:, None] / length - np.arange(grid)[None, :] / grid
    orders = np.arange(1, band)
    interp = (1 + 2 * np.cos(2 * math.pi * turn[:, :, None] * orders).sum(-1)) / grid
    ih, il = halves(interp)
    gap = np.zeros((tile, WIDE - grid), ih.dtype)
    wn = np.concatenate([ih, gap, ih, gap, il, gap, il, gap], 1)
    wt = np.concatenate([ih.T, il.T], 0)

    plus, minus = np.zeros((HALF, band)), np.zeros((HALF, band))
    for m in range(top):
        plus[spread(m), top + m] = 1
    for m in range(1, top + 1):
        minus[spread(m), top - m] = 1
    even, odd = plus + minus, plus - minus
    kl = np.concatenate([even, even, -odd, odd], 0)
    kr = np.stack([
        place(
            band, 2 * LANES,
            (0, SLOT * j, even.T), (0, SLOT * j + HALF, even.T),
            (0, LANES + SLOT * j, -odd.T), (0, LANES + SLOT * j + HALF, odd.T),
        )
        for j in range(SLOTS)
    ])
    front = dict(
        fcol=fcol, frow=frow, kr=kr.astype(BF), kl=kl.astype(BF),
        left=np.concatenate([sh, sh, sl], 1),
        th=th, tl=tl, wt=wt, wn=wn,
        tb=np.concatenate([th.T, tl.T], 1),
        lt=np.concatenate([bh.T, bh.T, bl.T], 1),
    )
    edge, mid = [0, SLOT], [SLOT, 2 * SLOT]
    rows = np.zeros((tile, 6 * SLOT), fh.dtype)
    for lo, hi, cut in ((0, margin, 0), (tile - margin, tile, SLOT)):
        pick = slice(cut, cut + 2 * SLOT)
        rows[lo:hi] = np.concatenate([fh[lo:hi, pick], fh[lo:hi, pick], fl[lo:hi, pick]], 1)
    lo, hi, pick = margin, tile - margin, slice(SLOT, 2 * SLOT)
    rows[lo:hi, : 3 * SLOT] = np.concatenate([fh[lo:hi, pick], fh[lo:hi, pick], fl[lo:hi, pick]], 1)
    back = dict(frow=frow, brow=rows)
    return front, back, grid


def split(x):
    high = x.astype(BF)
    return high, (x - high.astype(F32)).astype(BF)


def mm(a, b):
    return jnp.dot(a, b, preferred_element_type=F32)


def both_sides(rows, high, low, cols):
    n, m = rows.shape[0] // 2, cols.shape[1] // 2
    q = mm(rows, high)
    q = q[:n] + q[n:] + mm(rows[:n], low)
    out = mm(jnp.concatenate(split(q), 0), cols)
    return out[:n, :m] + out[:n, m:] + out[n:, :m]


def roll(x, shift):
    shift = shift % LANES
    return x if shift == 0 else pltpu.roll(x, shift, 1)


def by_slot(pieces):
    lane = lax.broadcasted_iota(jnp.int32, pieces[0].shape, 1)
    out = pieces[-1]
    for j in range(len(pieces) - 2, -1, -1):
        out = jnp.where(lane < (j + 1) * SLOT, pieces[j], out)
    return out


def swap(x):
    return jnp.concatenate([x[HALF:], x[:HALF]], 0)


def neighbours(ty, tx, n_ty, n_tx):
    here = (0, None, 0)
    if n_ty == 2:
        vert = [here, (1 - 2 * ty, None, 1)]
    else:
        vert = [here, (-1, ty > 0, 2), (1, ty < n_ty - 1, 1)][: 1 if n_ty == 1 else 3]
    side = [here, (-1, tx > 0, 2), (1, tx < n_tx - 1, 1)]
    spots = [(v, h) for v in range(len(vert)) for h in range(len(side))]

    def groups(mirror):
        out = {}
        for v, h in spots:
            keys = (vert[v][2], side[h][2]) if mirror else (v, h)
            key = (keys[0] if vert[v][1] is not None else 0, keys[1])
            out.setdefault(key, []).append((v, h))
        for (v, h), members in reversed(out.items()):
            tests = [t for t in (vert[v][1], side[h][1]) if t is not None]
            ok = None if not tests else tests[0] if len(tests) == 1 else tests[0] & tests[1]
            yield ok, members[::-1]

    return vert, side, spots, groups


def front_kernel(names, grid, n_k, *refs):
    n_tab = len(names)
    logits_hbm, target_hbm, weight_hbm, kern_hbm = refs[:4]
    tab_hbm = dict(zip(names, refs[4 : 4 + n_tab]))
    late_hbm = refs[4 + n_tab]
    out_ref, logits, fac, frow, late = refs[5 + n_tab : 10 + n_tab]
    rest = refs[10 + n_tab :]
    target, weight, kern = rest[:3]
    own = [n for n in names if n != "frow"]
    tab = dict(zip(own, rest[3 : 3 + len(own)]), frow=frow)
    (kq, send1, recv1, zs_own, recv2, level, signed,
     load_sem, s1, r1, s2, r2, ready) = rest[3 + len(own) :]

    tile = logits.shape[0]
    band = kern.shape[-1]
    n_g = n_k // SLOTS
    length = tile + 2 * MARGIN
    norm = 1.0 / (length * length)
    chunk = min(tile, 512)
    parts = [slice(i, i + chunk) for i in range(0, tile, chunk)]
    n_ty, n_tx, n_c = lax.axis_size("ty"), lax.axis_size("tx"), lax.axis_size("cond")
    ty, tx, me = lax.axis_index("ty"), lax.axis_index("tx"), lax.axis_index("cond")

    vert, side, spots, groups = neighbours(ty, tx, n_ty, n_tx)

    def target_of(spot, turn=0):
        v, h = spot
        where = {"ty": ty + vert[v][0], "tx": tx + side[h][0]}
        away = not isinstance(turn, int) or turn
        return dict(where, cond=lax.rem(me + turn, n_c)) if away else where

    def each(mirror, turns, act):
        for ok, members in groups(mirror):
            jobs_here = [(m, t) for m in members for t in turns if m != (0, 0) or not isinstance(t, int) or t]

            def run(jobs_here=jobs_here):
                for spot, turn in jobs_here:
                    act(spot, turn)

            if not jobs_here:
                continue
            if ok is None:
                run()
            else:
                pl.when(ok)(run)

    barrier = pltpu.get_barrier_semaphore()
    def greet(turns):
        each(False, turns, lambda spot, turn: pl.semaphore_signal(
            barrier, inc=1, device_id=target_of(spot, turn), device_id_type=MESH
        ))

    greet((0,))
    jobs = [("fcol", tab_hbm["fcol"], tab["fcol"])]
    jobs += [(part.start, logits_hbm.at[part], logits.at[part]) for part in parts]
    jobs += [("frow", tab_hbm["frow"], frow), ("kern", kern_hbm, kern)]
    jobs += [(n, tab_hbm[n], tab[n]) for n in ("kr", "kl")]
    jobs += [("target", target_hbm, target), ("weight", weight_hbm, weight)]
    jobs += [(n, tab_hbm[n], tab[n]) for n in own if n not in ("fcol", "kr", "kl")]
    jobs += [("late", late_hbm, late)]
    loads = {}
    for i, (name, source, dest) in enumerate(jobs):
        loads[name] = pltpu.make_async_copy(source, dest, load_sem.at[i])
        loads[name].start()

    for turn in range(1, n_c):
        pl.when(me + turn < n_c)(functools.partial(greet, (turn,)))
    for ok, members in groups(True):
        if ok is None:
            continue

        @pl.when(jnp.logical_not(ok))
        def _():
            for spot in members:
                recv1[spots.index(spot)] = jnp.zeros(recv1.shape[1:], F32)
                for turn in range(n_c):
                    recv2[turn, spots.index(spot)] = jnp.zeros(recv2.shape[2:], F32)

    loads["fcol"].wait()
    loads["frow"].wait()
    loads[0].wait()
    share = both_sides(frow[...], *split(0.5 + 0.5 * jnp.tanh(logits[...])), tab["fcol"][...])
    strips = {0: share[SLOT : 2 * SLOT]}
    for v in range(1, len(vert)):
        above, below = share[:SLOT], share[2 * SLOT :]
        dr = vert[v][0]
        strips[v] = (above if dr < 0 else below) if isinstance(dr, int) else jnp.where(dr < 0, above, below)
    for i, (v, h) in enumerate(spots):
        send1[i] = by_slot(
            [roll(strips[v][8 * t : 8 * t + 8], SLOT * (t - side[h][0] - 1)) for t in range(SLOTS)]
        )[:USED]

    plane = 0
    for ok, members in groups(True):
        plane = plane + len(members) * (1 if ok is None else ok.astype(jnp.int32))
    pl.semaphore_wait(barrier, plane - 1 + plane * me)

    def first(spot, turn=0):
        i = spots.index(spot)
        return pltpu.make_async_remote_copy(
            src_ref=send1.at[i], dst_ref=recv1.at[i], send_sem=s1.at[i], recv_sem=r1.at[i],
            device_id=target_of(spot), device_id_type=MESH,
        )

    def second(spot, turn):
        i = spots.index(spot)
        return pltpu.make_async_remote_copy(
            src_ref=zs_own, dst_ref=recv2.at[turn, i], send_sem=s2.at[turn, i],
            recv_sem=r2.at[turn, i], device_id=target_of(spot, turn), device_id_type=MESH,
        )

    each(False, (0,), lambda spot, turn: first(spot).start())

    def answer(turn):
        each(False, (turn,), lambda spot, turn: pl.semaphore_signal(
            ready, inc=1, device_id=target_of(spot, turn), device_id_type=MESH
        ))

    for back in range(1, n_c):
        pl.when(me >= back)(functools.partial(answer, n_c - back))

    for name in ("kern", "kr", "kl"):
        loads[name].wait()
    turned = None
    for j in range(SLOTS):
        rows = jnp.concatenate(
            [kern[0, SLOTS * g + j, ri] for g in range(n_g) for ri in range(2)], 0
        )
        high, low = split(rows)
        piece = mm(high, tab["kr"][j]) + mm(low, tab["kr"][j])
        turned = piece if turned is None else turned + piece
    for e in range(2 * n_g):
        high, low = split(turned[e * band : (e + 1) * band])
        kq[:, 2 * LANES * e : 2 * LANES * (e + 1)] = mm(tab["kl"][...], high) + mm(tab["kl"][...], low)
    loads["target"].wait()
    loads["weight"].wait()

    def prepare(i, carry):
        part = pl.ds(pl.multiple_of(i * 32, 32), 32)
        vals = weight[part].astype(F32)
        level[part] = vals
        signed[part] = vals * (2.0 * target[part].astype(F32) - 1.0)
        mask = jnp.tanh(logits[part])
        fac[part] = (1.5 * STEP_SIZE * norm) * (mask * mask - 1.0)
        return carry

    lax.fori_loop(0, tile // 32, prepare, 0)
    for name in own:
        if name not in ("fcol", "kr", "kl"):
            loads[name].wait()
    loads["late"].wait()

    each(True, (0,), lambda spot, turn: first(spot).wait_recv())
    spec = send1[0]
    for i in range(1, len(spots)):
        spec = spec + recv1[i]
    rest8 = jnp.zeros((8 - USED, LANES), F32)
    spec = jnp.concatenate([spec, rest8], 0)

    turns = [roll(spec, SLOT * s) for s in range(SLOTS)]
    u = jnp.concatenate(
        [by_slot([turns[(j - t) % SLOTS] for j in range(SLOTS)]) for t in range(SLOTS)], 0
    )
    v = roll(u, HALF)
    us, vs = swap(u), swap(v)

    def quarter(e, row, col):
        left = 2 * LANES * e + LANES * col
        return kq[SLOT * row : SLOT * (row + 1), left : left + LANES]

    coef = []
    for g in range(n_g):
        r, i = 2 * g, 2 * g + 1
        coef.append(quarter(r, 0, 0) * u - quarter(r, 1, 1) * vs - quarter(i, 1, 0) * us - quarter(i, 0, 1) * v)
        coef.append(quarter(i, 0, 0) * u - quarter(i, 1, 1) * vs + quarter(r, 1, 0) * us + quarter(r, 0, 1) * v)
    n_e = 2 * n_g
    ah, al = split(jnp.concatenate(coef, 1))
    half = mm(tab["left"][...], jnp.concatenate([ah, al, ah], 0))
    hh, hl = split(jnp.concatenate([half[:, LANES * e : LANES * (e + 1)] for e in range(n_e)], 0))
    field = mm(hh, tab["th"][...]) + mm(hl, tab["th"][...]) + mm(hh, tab["tl"][...])
    coarse = jnp.zeros((grid, 2 * LANES), F32)
    for e in range(n_e):
        cut = field[grid * e : grid * (e + 1)]
        coarse = coarse + cut * cut
    coarse = coarse[:, :LANES] + coarse[:, LANES:]
    coarse = (0.5 * STEEPNESS) * (coarse + roll(coarse, WIDE) - THRESHOLD)
    ch, cl = split(coarse[:, :grid])
    wt = tab["wt"]
    uh, ul = split(mm(ch, wt[:grid]) + mm(cl, wt[:grid]) + mm(ch, wt[grid:]))
    gap = jnp.zeros((WIDE - grid, tile), BF)
    ustack = jnp.concatenate([uh, gap, ul, gap, uh, gap, gap, gap, gap, gap], 0)[: 4 * WIDE]

    gsum = None
    for part in [slice(0, tile)]:
        th = jnp.tanh(mm(tab["wn"][part], ustack))
        gain = (level[part] * th - signed[part]) * (1.0 - th * th)
        gh, gl = split(gain)
        wide = mm(gh, tab["wn"][...])
        y = wide[:, :LANES] + wide[:, LANES:] + mm(gl, tab["wn"][:, :LANES])
        piece = mm(wt[:, part], jnp.concatenate(split(y), 1))
        gsum = piece if gsum is None else gsum + piece
    gcoarse = gsum[:grid, :LANES] + gsum[:grid, LANES:] + gsum[grid:, :LANES]

    gpair = jnp.concatenate([gcoarse, gcoarse], 1)
    dh, dl = split(jnp.concatenate([gpair * field[grid * e : grid * (e + 1)] for e in range(n_e)], 0))
    wide = mm(dh, tab["tb"][...])
    down = wide[:, :LANES] + wide[:, LANES:] + mm(dl, tab["tb"][:, :LANES])
    eh, el = split(jnp.concatenate([down[grid * e : grid * (e + 1)] for e in range(n_e)], 1))
    d = mm(tab["lt"][...], jnp.concatenate([eh, el, eh], 0))
    du = jnp.zeros((SLOT, LANES), F32)
    dus, dv, dvs = du, du, du
    for g in range(n_g):
        r, i = 2 * g, 2 * g + 1
        dr_, di_ = d[:, LANES * r : LANES * (r + 1)], d[:, LANES * i : LANES * (i + 1)]
        du = du + quarter(r, 0, 0) * dr_ + quarter(i, 0, 0) * di_
        dus = dus + quarter(r, 1, 0) * di_ - quarter(i, 1, 0) * dr_
        dv = dv + quarter(r, 0, 1) * di_ - quarter(i, 0, 1) * dr_
        dvs = dvs - quarter(r, 1, 1) * dr_ - quarter(i, 1, 1) * di_
    dx = du + swap(dus) + roll(dv + swap(dvs), HALF)
    x = [dx[8 * t : 8 * t + 8] for t in range(SLOTS)]
    lane = lax.broadcasted_iota(jnp.int32, (8, LANES), 1)
    even, low = (lane // SLOT) % 2 == 0, lane < 2 * SLOT
    pair = [
        jnp.where(even, a, b) + jnp.where(
            even, roll(jnp.where(even, b, a), -SLOT), roll(jnp.where(even, b, a), SLOT)
        )
        for a, b in ((x[0], x[1]), (x[2], x[3]))
    ]
    zs = jnp.where(low, pair[0], pair[1]) + roll(jnp.where(low, pair[1], pair[0]), 2 * SLOT)
    zs_own[...] = zs[:USED]

    @pl.when(me < n_c - 1)
    def _():
        pl.semaphore_wait(ready, plane * (n_c - 1 - me))

    high = (2 * me >= n_c).astype(jnp.int32)
    for k in range(n_c - 1):
        up = k + (k >= me).astype(jnp.int32)
        down = n_c - 1 - k - (n_c - 1 - k <= me).astype(jnp.int32)
        goal = high * up + (1 - high) * down
        turn = lax.rem(goal - me + n_c, n_c)
        each(False, (turn,), lambda spot, turn: second(spot, turn).start())
    each(False, (0,), lambda spot, turn: second(spot, turn).start())
    recv2[0, 0] = zs_own[...]
    each(True, range(n_c), lambda spot, turn: second(spot, turn).wait_recv())
    blocks = {}
    for i, (v, h) in enumerate(spots):
        total = recv2[0, i]
        for turn in range(1, n_c):
            total = total + recv2[turn, i]
        blocks[v, h] = jnp.concatenate([total, rest8], 0)
    bands = []
    for v in range(len(vert)):
        line = [blocks[v, h] for h in (2, 0, 1)]
        bands.append(jnp.concatenate(
            [by_slot([roll(b, SLOT * (i - t)) for i, b in enumerate(line)]) for t in range(SLOTS)], 0
        ))
    none = jnp.zeros((SLOT, LANES), F32)
    if len(vert) == 1:
        above = below = none
    elif len(vert) == 2:
        above = jnp.where(vert[1][0] < 0, bands[1], none)
        below = jnp.where(vert[1][0] < 0, none, bands[1])
    else:
        above, below = bands[2], bands[1]
    out_ref[:SLOT] = above
    out_ref[SLOT : 2 * SLOT] = bands[0]
    out_ref[2 * SLOT :] = below

    each(False, (0,), lambda spot, turn: first(spot).wait_send())
    each(False, range(n_c), lambda spot, turn: second(spot, turn).wait_send())


def back_kernel(z_ref, logits, fac, frow, brow, new_hbm, next_hbm, new, nxt, sem):
    tile = logits.shape[1]
    n_f = 3 * SLOT
    zh, zl = split(z_ref[:, :n_f])
    w = mm(zh, frow[:n_f]) + mm(zl, frow[:n_f]) + mm(zh, frow[n_f:])
    wh, wl = split(w)

    chunk = min(MARGIN, 128)
    copies = []
    for i in range(tile // chunk):
        lo, hi = i * chunk, (i + 1) * chunk
        part = slice(lo, hi)
        first = 0 if lo < MARGIN else SLOT
        last = 3 * SLOT if hi > tile - MARGIN else 2 * SLOT
        pick = slice(first, last)
        stack = jnp.concatenate([wh[pick], wl[pick], wh[pick]], 0)
        grad = mm(brow[part, : 3 * (last - first)], stack)
        value = logits[part] + fac[part] * grad
        new[part] = value
        nxt[part] = (0.5 + 0.5 * jnp.tanh(value)).astype(BF)
        for j, (buf, out) in enumerate(((new, new_hbm), (nxt, next_hbm))):
            copy = pltpu.make_async_copy(buf.at[part], out.at[part], sem.at[2 * i + j])
            copy.start()
            copies.append(copy)
    for copy in copies:
        copy.wait()


def per_device(mask_logits, target_layout, density_weights, socs_kernels):
    tile = mask_logits.shape[0]
    band = socs_kernels.shape[-1]
    n_k = socs_kernels.shape[1]
    assert n_k % SLOTS == 0
    n_c, n_ty = lax.axis_size("cond"), lax.axis_size("ty")
    front, back, grid = make_tables(tile, MARGIN, band)
    names = list(front)
    arrays = [mask_logits, target_layout, density_weights, socs_kernels]
    tables = {n: jnp.asarray(front[n]) for n in names}
    late = jnp.asarray(back["brow"])
    in_vmem = pl.BlockSpec(memory_space=pltpu.VMEM)
    in_hbm = pl.BlockSpec(memory_space=pl.ANY)
    vmem = lambda a: pltpu.VMEM(a.shape, a.dtype)
    dma = pltpu.SemaphoreType.DMA
    n_off = 3 * min(n_ty, 3)
    held = (USED, LANES)
    n_load = len(names) + 5 + tile // min(tile, 512)
    operands = arrays + [tables[n] for n in names] + [late]
    kept = pl.pallas_call(
        functools.partial(front_kernel, names, grid, n_k),
        out_shape=[
            pltpu.VMEM((3 * SLOT, LANES), F32), pltpu.VMEM((tile, tile), F32),
            pltpu.VMEM((tile, tile), F32), vmem(tables["frow"]), vmem(late),
        ],
        in_specs=[in_hbm] * len(operands),
        out_specs=[in_vmem] * 5,
        scratch_shapes=[vmem(a) for a in arrays[1:]]
        + [vmem(tables[n]) for n in names if n != "frow"]
        + [
            pltpu.VMEM((2 * SLOT, 2 * LANES * 2 * n_k // SLOTS), F32),
            pltpu.VMEM((n_off, *held), F32),
            pltpu.VMEM((n_off, *held), F32),
            pltpu.VMEM(held, F32),
            pltpu.VMEM((n_c, n_off, *held), F32),
            pltpu.VMEM((tile, tile), F32),
            pltpu.VMEM((tile, tile), F32),
            dma((n_load,)),
            dma((n_off,)),
            dma((n_off,)),
            dma((n_c, n_off)),
            dma((n_c, n_off)),
            pltpu.SemaphoreType.REGULAR,
        ],
        compiler_params=pltpu.CompilerParams(
            collective_id=0, has_side_effects=True, vmem_limit_bytes=56 * 2**20
        ),
    )(*operands)

    return pl.pallas_call(
        back_kernel,
        out_shape=(
            jax.ShapeDtypeStruct((tile, tile), F32),
            jax.ShapeDtypeStruct((tile, tile), BF),
        ),
        in_specs=[in_vmem] * 5,
        out_specs=(in_hbm, in_hbm),
        scratch_shapes=[
            pltpu.VMEM((tile, tile), F32),
            pltpu.VMEM((tile, tile), BF),
            dma((2 * (tile // min(MARGIN, 128)),)),
        ],
        compiler_params=pltpu.CompilerParams(vmem_limit_bytes=16 * 2**20),
    )(*kept)


def solution(mesh):
    in_specs = (P("ty", "tx"), P("ty", "tx"), P("ty", "tx"), P("cond", None, None, None, None))
    out_specs = (P("ty", "tx"), P("ty", "tx"))
    return jax.shard_map(
        per_device, mesh=mesh, in_specs=in_specs, out_specs=out_specs, check_vma=False
    )
```

```python
import functools
import math

import jax
import jax.numpy as jnp
import numpy as np
from jax import lax
from jax.experimental import pallas as pl
from jax.experimental.pallas import tpu as pltpu
from jax.sharding import PartitionSpec as P

MARGIN = 128
STEEPNESS = 6.0
THRESHOLD = 0.25
STEP_SIZE = 4.0
LANES = 128
HALF = 16
USED = 7
SLOT = 2 * HALF
SLOTS = LANES // SLOT
WIDE = 64
MESH = pl.DeviceIdType.MESH
BF = jnp.bfloat16
F32 = jnp.float32


def halves(table):
    table = np.asarray(table, np.float32)
    high = table.astype(BF)
    return high, (table - high.astype(np.float32)).astype(BF)


def place(rows, cols, *pieces):
    out = np.zeros((rows, cols))
    for top, left, piece in pieces:
        out[top : top + piece.shape[0], left : left + piece.shape[1]] = piece
    return out


def spread(order):
    return order + order // USED


def trig(positions, top, period):
    turns = np.mod(np.outer(positions, np.arange(top + 1)), period).astype(np.float64)
    angle = turns * (2 * math.pi / period)
    out = np.zeros((len(positions), SLOT))
    out[:, spread(np.arange(top + 1))] = np.cos(angle)
    out[:, HALF + spread(np.arange(top + 1))] = np.sin(angle)
    return out


def make_tables(tile, margin, band):
    top = band // 2
    assert band % 2 == 0 and spread(top) < HALF and tile >= 2 * margin
    length = tile + 2 * margin
    grid = -(-(2 * band - 1) // 16) * 16
    assert grid <= WIDE
    shifted = []
    for step in (-1, 0, 1):
        spots = np.arange(tile) + margin - step * tile
        inside = ((spots >= 0) & (spots < length))[:, None]
        shifted.append(trig(spots, top, length) * inside)
    wave = np.concatenate(shifted, 1)
    fh, fl = halves(wave)
    pad = np.zeros((tile, LANES - 3 * SLOT), fh.dtype)
    fcol = np.concatenate([fh, pad, fl, pad], 1)
    frow = np.concatenate([fh.T, fl.T], 0)

    ec = trig(np.arange(grid), top, grid)
    bh, bl = halves(ec)
    norm = 1.0 / (length * length)
    sh, sl = halves(ec * norm)
    block = place(LANES, SLOTS * WIDE, *((SLOT * j, WIDE * j, ec.T) for j in range(SLOTS)))
    th, tl = halves(block)
    turn = (np.arange(tile) + margin)[:, None] / length - np.arange(grid)[None, :] / grid
    orders = np.arange(1, band)
    interp = (1 + 2 * np.cos(2 * math.pi * turn[:, :, None] * orders).sum(-1)) / grid
    ih, il = halves(interp)
    gap = np.zeros((tile, WIDE - grid), ih.dtype)
    wn = np.concatenate([ih, gap, ih, gap, il, gap, il, gap], 1)
    wt = np.concatenate([ih.T, il.T], 0)

    plus, minus = np.zeros((HALF, band)), np.zeros((HALF, band))
    for m in range(top):
        plus[spread(m), top + m] = 1
    for m in range(1, top + 1):
        minus[spread(m), top - m] = 1
    even, odd = plus + minus, plus - minus
    kl = np.concatenate([even, even, -odd, odd], 0)
    kr = np.stack([
        place(
            band, 2 * LANES,
            (0, SLOT * j, even.T), (0, SLOT * j + HALF, even.T),
            (0, LANES + SLOT * j, -odd.T), (0, LANES + SLOT * j + HALF, odd.T),
        )
        for j in range(SLOTS)
    ])
    front = dict(
        fcol=fcol, frow=frow, kr=kr.astype(BF), kl=kl.astype(BF),
        left=np.concatenate([sh, sh, sl], 1),
        th=th, tl=tl, wt=wt, wn=wn,
        tb=np.concatenate([th.T, tl.T], 1),
        lt=np.concatenate([bh.T, bh.T, bl.T], 1),
    )
    edge, mid = [0, SLOT], [SLOT, 2 * SLOT]
    rows = np.zeros((tile, 6 * SLOT), fh.dtype)
    for lo, hi, cut in ((0, margin, 0), (tile - margin, tile, SLOT)):
        pick = slice(cut, cut + 2 * SLOT)
        rows[lo:hi] = np.concatenate([fh[lo:hi, pick], fh[lo:hi, pick], fl[lo:hi, pick]], 1)
    lo, hi, pick = margin, tile - margin, slice(SLOT, 2 * SLOT)
    rows[lo:hi, : 3 * SLOT] = np.concatenate([fh[lo:hi, pick], fh[lo:hi, pick], fl[lo:hi, pick]], 1)
    back = dict(frow=frow, brow=rows)
    return front, back, grid


def split(x):
    high = x.astype(BF)
    return high, (x - high.astype(F32)).astype(BF)


def mm(a, b):
    return jnp.dot(a, b, preferred_element_type=F32)


def both_sides(rows, high, low, cols):
    n, m = rows.shape[0] // 2, cols.shape[1] // 2
    q = mm(rows, high)
    q = q[:n] + q[n:] + mm(rows[:n], low)
    out = mm(jnp.concatenate(split(q), 0), cols)
    return out[:n, :m] + out[:n, m:] + out[n:, :m]


def roll(x, shift):
    shift = shift % LANES
    return x if shift == 0 else pltpu.roll(x, shift, 1)


def by_slot(pieces):
    lane = lax.broadcasted_iota(jnp.int32, pieces[0].shape, 1)
    out = pieces[-1]
    for j in range(len(pieces) - 2, -1, -1):
        out = jnp.where(lane < (j + 1) * SLOT, pieces[j], out)
    return out


def swap(x):
    return jnp.concatenate([x[HALF:], x[:HALF]], 0)


def neighbours(ty, tx, n_ty, n_tx):
    here = (0, None, 0)
    if n_ty == 2:
        vert = [here, (1 - 2 * ty, None, 1)]
    else:
        vert = [here, (-1, ty > 0, 2), (1, ty < n_ty - 1, 1)][: 1 if n_ty == 1 else 3]
    side = [here, (-1, tx > 0, 2), (1, tx < n_tx - 1, 1)]
    spots = [(v, h) for v in range(len(vert)) for h in range(len(side))]

    def groups(mirror):
        out = {}
        for v, h in spots:
            keys = (vert[v][2], side[h][2]) if mirror else (v, h)
            key = (keys[0] if vert[v][1] is not None else 0, keys[1])
            out.setdefault(key, []).append((v, h))
        for (v, h), members in reversed(out.items()):
            tests = [t for t in (vert[v][1], side[h][1]) if t is not None]
            ok = None if not tests else tests[0] if len(tests) == 1 else tests[0] & tests[1]
            yield ok, members[::-1]

    return vert, side, spots, groups


def front_kernel(names, grid, n_k, *refs):
    n_tab = len(names)
    logits_hbm, target_hbm, weight_hbm, kern_hbm = refs[:4]
    tab_hbm = dict(zip(names, refs[4 : 4 + n_tab]))
    late_hbm = refs[4 + n_tab]
    out_ref, logits, fac, frow, late = refs[5 + n_tab : 10 + n_tab]
    rest = refs[10 + n_tab :]
    target, weight, kern = rest[:3]
    own = [n for n in names if n != "frow"]
    tab = dict(zip(own, rest[3 : 3 + len(own)]), frow=frow)
    (kq, send1, recv1, zs_own, recv2, level, signed,
     load_sem, s1, r1, s2, r2, ready) = rest[3 + len(own) :]

    tile = logits.shape[0]
    band = kern.shape[-1]
    n_g = n_k // SLOTS
    length = tile + 2 * MARGIN
    norm = 1.0 / (length * length)
    chunk = tile // 4
    parts = [slice(i, i + chunk) for i in range(0, tile, chunk)]
    n_ty, n_tx, n_c = lax.axis_size("ty"), lax.axis_size("tx"), lax.axis_size("cond")
    ty, tx, me = lax.axis_index("ty"), lax.axis_index("tx"), lax.axis_index("cond")

    vert, side, spots, groups = neighbours(ty, tx, n_ty, n_tx)

    def target_of(spot, turn=0):
        v, h = spot
        where = {"ty": ty + vert[v][0], "tx": tx + side[h][0]}
        away = not isinstance(turn, int) or turn
        return dict(where, cond=lax.rem(me + turn, n_c)) if away else where

    def each(mirror, turns, act):
        for ok, members in groups(mirror):
            jobs_here = [(m, t) for m in members for t in turns if m != (0, 0) or not isinstance(t, int) or t]

            def run(jobs_here=jobs_here):
                for spot, turn in jobs_here:
                    act(spot, turn)

            if not jobs_here:
                continue
            if ok is None:
                run()
            else:
                pl.when(ok)(run)

    barrier = pltpu.get_barrier_semaphore()
    def greet(turns):
        each(False, turns, lambda spot, turn: pl.semaphore_signal(
            barrier, inc=1, device_id=target_of(spot, turn), device_id_type=MESH
        ))

    jobs = [(part.start, logits_hbm.at[part], logits.at[part]) for part in parts]
    jobs += [("frow", tab_hbm["frow"], frow), ("fcol", tab_hbm["fcol"], tab["fcol"]), ("kern", kern_hbm, kern)]
    jobs += [(n, tab_hbm[n], tab[n]) for n in ("kr", "kl")]
    jobs += [("target", target_hbm, target), ("weight", weight_hbm, weight)]
    jobs += [(n, tab_hbm[n], tab[n]) for n in own if n not in ("fcol", "kr", "kl")]
    jobs += [("late", late_hbm, late)]
    loads = {}
    for i, (name, source, dest) in enumerate(jobs):
        loads[name] = pltpu.make_async_copy(source, dest, load_sem.at[i])
        loads[name].start()
        if name == "fcol":
            greet((0,))

    for turn in range(1, n_c):
        pl.when(me + turn < n_c)(functools.partial(greet, (turn,)))
    for ok, members in groups(True):
        if ok is None:
            continue

        @pl.when(jnp.logical_not(ok))
        def _():
            for spot in members:
                recv1[spots.index(spot)] = jnp.zeros(recv1.shape[1:], F32)
                for turn in range(n_c):
                    recv2[turn, spots.index(spot)] = jnp.zeros(recv2.shape[2:], F32)

    loads["fcol"].wait()
    for part in parts:
        loads[part.start].wait()
    loads["frow"].wait()
    share = both_sides(frow[...], *split(0.5 + 0.5 * jnp.tanh(logits[...])), tab["fcol"][...])
    strips = {0: share[SLOT : 2 * SLOT]}
    for v in range(1, len(vert)):
        above, below = share[:SLOT], share[2 * SLOT :]
        dr = vert[v][0]
        strips[v] = (above if dr < 0 else below) if isinstance(dr, int) else jnp.where(dr < 0, above, below)
    for i, (v, h) in enumerate(spots):
        send1[i] = by_slot(
            [roll(strips[v][8 * t : 8 * t + 8], SLOT * (t - side[h][0] - 1)) for t in range(SLOTS)]
        )[:USED]

    plane = 0
    for ok, members in groups(True):
        plane = plane + len(members) * (1 if ok is None else ok.astype(jnp.int32))
    pl.semaphore_wait(barrier, plane - 1 + plane * me)

    def first(spot, turn=0):
        i = spots.index(spot)
        return pltpu.make_async_remote_copy(
            src_ref=send1.at[i], dst_ref=recv1.at[i], send_sem=s1.at[i], recv_sem=r1.at[i],
            device_id=target_of(spot), device_id_type=MESH,
        )

    def second(spot, turn):
        i = spots.index(spot)
        return pltpu.make_async_remote_copy(
            src_ref=zs_own, dst_ref=recv2.at[turn, i], send_sem=s2.at[turn, i],
            recv_sem=r2.at[turn, i], device_id=target_of(spot, turn), device_id_type=MESH,
        )

    each(False, (0,), lambda spot, turn: first(spot).start())

    def answer(turn):
        each(False, (turn,), lambda spot, turn: pl.semaphore_signal(
            ready, inc=1, device_id=target_of(spot, turn), device_id_type=MESH
        ))

    for back in range(1, n_c):
        pl.when(me >= back)(functools.partial(answer, n_c - back))

    for name in ("kern", "kr", "kl"):
        loads[name].wait()
    turned = None
    for j in range(SLOTS):
        rows = jnp.concatenate(
            [kern[0, SLOTS * g + j, ri] for g in range(n_g) for ri in range(2)], 0
        )
        high, low = split(rows)
        piece = mm(high, tab["kr"][j]) + mm(low, tab["kr"][j])
        turned = piece if turned is None else turned + piece
    for e in range(2 * n_g):
        high, low = split(turned[e * band : (e + 1) * band])
        kq[:, 2 * LANES * e : 2 * LANES * (e + 1)] = mm(tab["kl"][...], high) + mm(tab["kl"][...], low)
    loads["target"].wait()
    loads["weight"].wait()

    def prepare(i, carry):
        part = pl.ds(pl.multiple_of(i * 32, 32), 32)
        vals = weight[part].astype(F32)
        level[part] = vals
        signed[part] = vals * (2.0 * target[part].astype(F32) - 1.0)
        mask = jnp.tanh(logits[part])
        fac[part] = (1.5 * STEP_SIZE * norm) * (mask * mask - 1.0)
        return carry

    lax.fori_loop(0, tile // 32, prepare, 0)
    for name in own:
        if name not in ("fcol", "kr", "kl"):
            loads[name].wait()
    loads["late"].wait()

    each(False, (0,), lambda spot, turn: first(spot).wait_send())
    each(True, (0,), lambda spot, turn: first(spot).wait_recv())
    spec = send1[0]
    for i in range(1, len(spots)):
        spec = spec + recv1[i]
    rest8 = jnp.zeros((8 - USED, LANES), F32)
    spec = jnp.concatenate([spec, rest8], 0)

    turns = [roll(spec, SLOT * s) for s in range(SLOTS)]
    u = jnp.concatenate(
        [by_slot([turns[(j - t) % SLOTS] for j in range(SLOTS)]) for t in range(SLOTS)], 0
    )
    v = roll(u, HALF)
    us, vs = swap(u), swap(v)

    def quarter(e, row, col):
        left = 2 * LANES * e + LANES * col
        return kq[SLOT * row : SLOT * (row + 1), left : left + LANES]

    coef = []
    for g in range(n_g):
        r, i = 2 * g, 2 * g + 1
        coef.append(quarter(r, 0, 0) * u - quarter(r, 1, 1) * vs - quarter(i, 1, 0) * us - quarter(i, 0, 1) * v)
        coef.append(quarter(i, 0, 0) * u - quarter(i, 1, 1) * vs + quarter(r, 1, 0) * us + quarter(r, 0, 1) * v)
    n_e = 2 * n_g
    ah, al = split(jnp.concatenate(coef, 1))
    half = mm(tab["left"][...], jnp.concatenate([ah, al, ah], 0))
    hh, hl = split(jnp.concatenate([half[:, LANES * e : LANES * (e + 1)] for e in range(n_e)], 0))
    th, tl = tab["th"][...], tab["tl"][...]
    field = mm(jnp.concatenate([hh, hl, hh], 1), jnp.concatenate([th, th, tl], 0))
    coarse = jnp.zeros((grid, 2 * LANES), F32)
    for e in range(n_e):
        cut = field[grid * e : grid * (e + 1)]
        coarse = coarse + cut * cut
    coarse = coarse[:, :LANES] + coarse[:, LANES:]
    lane = lax.broadcasted_iota(jnp.int32, coarse.shape, 1)
    coarse = (0.5 * STEEPNESS) * (coarse - jnp.where(lane < WIDE, THRESHOLD, 0.0))
    ch, cl = split(coarse)
    wt = tab["wt"]
    hole = jnp.zeros((WIDE - grid, tile), BF)
    wth, wtl = [wt[:grid], hole] * 2, [wt[grid:], hole] * 2
    uh, ul = split(mm(jnp.concatenate([ch, cl, ch], 1), jnp.concatenate(wth + wth + wtl, 0)))
    gap = jnp.zeros((WIDE - grid, tile), BF)
    ustack = jnp.concatenate([uh, gap, ul, gap, uh, gap, gap, gap, gap, gap], 0)[: 4 * WIDE]

    gsum = None
    for part in [slice(0, tile)]:
        th = jnp.tanh(mm(tab["wn"][part], ustack))
        gain = (level[part] * th - signed[part]) * (1.0 - th * th)
        gh, gl = split(gain)
        wide = mm(gh, tab["wn"][...])
        y = wide[:, :LANES] + wide[:, LANES:] + mm(gl, tab["wn"][:, :LANES])
        piece = mm(wt[:, part], jnp.concatenate(split(y), 1))
        gsum = piece if gsum is None else gsum + piece
    gcoarse = gsum[:grid, :LANES] + gsum[:grid, LANES:] + gsum[grid:, :LANES]

    gpair = jnp.concatenate([gcoarse, gcoarse], 1)
    dh, dl = split(jnp.concatenate([gpair * field[grid * e : grid * (e + 1)] for e in range(n_e)], 0))
    wide = mm(dh, tab["tb"][...])
    down = wide[:, :LANES] + wide[:, LANES:] + mm(dl, tab["tb"][:, :LANES])
    eh, el = split(jnp.concatenate([down[grid * e : grid * (e + 1)] for e in range(n_e)], 1))
    d = mm(tab["lt"][...], jnp.concatenate([eh, el, eh], 0))
    du = jnp.zeros((SLOT, LANES), F32)
    dus, dv, dvs = du, du, du
    for g in range(n_g):
        r, i = 2 * g, 2 * g + 1
        dr_, di_ = d[:, LANES * r : LANES * (r + 1)], d[:, LANES * i : LANES * (i + 1)]
        du = du + quarter(r, 0, 0) * dr_ + quarter(i, 0, 0) * di_
        dus = dus + quarter(r, 1, 0) * di_ - quarter(i, 1, 0) * dr_
        dv = dv + quarter(r, 0, 1) * di_ - quarter(i, 0, 1) * dr_
        dvs = dvs - quarter(r, 1, 1) * dr_ - quarter(i, 1, 1) * di_
    dx = du + swap(dus) + roll(dv + swap(dvs), HALF)
    x = [dx[8 * t : 8 * t + 8] for t in range(SLOTS)]
    lane = lax.broadcasted_iota(jnp.int32, (8, LANES), 1)
    even, low = (lane // SLOT) % 2 == 0, lane < 2 * SLOT
    pair = [
        jnp.where(even, a, b) + jnp.where(
            even, roll(jnp.where(even, b, a), -SLOT), roll(jnp.where(even, b, a), SLOT)
        )
        for a, b in ((x[0], x[1]), (x[2], x[3]))
    ]
    zs = jnp.where(low, pair[0], pair[1]) + roll(jnp.where(low, pair[1], pair[0]), 2 * SLOT)
    zs_own[...] = zs[:USED]

    @pl.when(me < n_c - 1)
    def _():
        pl.semaphore_wait(ready, plane * (n_c - 1 - me))

    high = (2 * me >= n_c).astype(jnp.int32)
    for k in range(n_c - 1):
        up = k + (k >= me).astype(jnp.int32)
        down = n_c - 1 - k - (n_c - 1 - k <= me).astype(jnp.int32)
        goal = high * up + (1 - high) * down
        turn = lax.rem(goal - me + n_c, n_c)
        each(False, (turn,), lambda spot, turn: second(spot, turn).start())
    each(False, (0,), lambda spot, turn: second(spot, turn).start())
    recv2[0, 0] = zs_own[...]
    each(False, range(n_c), lambda spot, turn: second(spot, turn).wait_send())
    each(True, range(n_c), lambda spot, turn: second(spot, turn).wait_recv())
    blocks = {}
    for i, (v, h) in enumerate(spots):
        total = recv2[0, i]
        for turn in range(1, n_c):
            total = total + recv2[turn, i]
        blocks[v, h] = jnp.concatenate([total, rest8], 0)
    bands = []
    for v in range(len(vert)):
        line = [blocks[v, h] for h in (2, 0, 1)]
        bands.append(jnp.concatenate(
            [by_slot([roll(b, SLOT * (i - t)) for i, b in enumerate(line)]) for t in range(SLOTS)], 0
        ))
    none = jnp.zeros((SLOT, LANES), F32)
    if len(vert) == 1:
        above = below = none
    elif len(vert) == 2:
        above = jnp.where(vert[1][0] < 0, bands[1], none)
        below = jnp.where(vert[1][0] < 0, none, bands[1])
    else:
        above, below = bands[2], bands[1]
    out_ref[:SLOT] = above
    out_ref[SLOT : 2 * SLOT] = bands[0]
    out_ref[2 * SLOT :] = below


def back_kernel(z_ref, logits, fac, frow, brow, new_hbm, next_hbm, new, nxt, sem):
    tile = logits.shape[1]
    n_f = 3 * SLOT
    zh, zl = split(z_ref[:, :n_f])
    w = mm(zh, frow[:n_f]) + mm(zl, frow[:n_f]) + mm(zh, frow[n_f:])
    wh, wl = split(w)

    chunk = min(MARGIN, 128)
    copies = []
    for i in range(tile // chunk):
        lo, hi = i * chunk, (i + 1) * chunk
        part = slice(lo, hi)
        first = 0 if lo < MARGIN else SLOT
        last = 3 * SLOT if hi > tile - MARGIN else 2 * SLOT
        pick = slice(first, last)
        stack = jnp.concatenate([wh[pick], wl[pick], wh[pick]], 0)
        grad = mm(brow[part, : 3 * (last - first)], stack)
        value = logits[part] + fac[part] * grad
        new[part] = value
        nxt[part] = (0.5 + 0.5 * jnp.tanh(value)).astype(BF)
        for j, (buf, out) in enumerate(((new, new_hbm), (nxt, next_hbm))):
            copy = pltpu.make_async_copy(buf.at[part], out.at[part], sem.at[2 * i + j])
            copy.start()
            copies.append(copy)
    for copy in copies:
        copy.wait()


def per_device(mask_logits, target_layout, density_weights, socs_kernels):
    tile = mask_logits.shape[0]
    band = socs_kernels.shape[-1]
    n_k = socs_kernels.shape[1]
    assert n_k % SLOTS == 0
    n_c, n_ty = lax.axis_size("cond"), lax.axis_size("ty")
    front, back, grid = make_tables(tile, MARGIN, band)
    names = list(front)
    arrays = [mask_logits, target_layout, density_weights, socs_kernels]
    tables = {n: jnp.asarray(front[n]) for n in names}
    late = jnp.asarray(back["brow"])
    in_vmem = pl.BlockSpec(memory_space=pltpu.VMEM)
    in_hbm = pl.BlockSpec(memory_space=pl.ANY)
    vmem = lambda a: pltpu.VMEM(a.shape, a.dtype)
    dma = pltpu.SemaphoreType.DMA
    n_off = 3 * min(n_ty, 3)
    held = (USED, LANES)
    n_load = len(names) + 5 + 4
    operands = arrays + [tables[n] for n in names] + [late]
    kept = pl.pallas_call(
        functools.partial(front_kernel, names, grid, n_k),
        out_shape=[
            pltpu.VMEM((3 * SLOT, LANES), F32), pltpu.VMEM((tile, tile), F32),
            pltpu.VMEM((tile, tile), F32), vmem(tables["frow"]), vmem(late),
        ],
        in_specs=[in_hbm] * len(operands),
        out_specs=[in_vmem] * 5,
        scratch_shapes=[vmem(a) for a in arrays[1:]]
        + [vmem(tables[n]) for n in names if n != "frow"]
        + [
            pltpu.VMEM((2 * SLOT, 2 * LANES * 2 * n_k // SLOTS), F32),
            pltpu.VMEM((n_off, *held), F32),
            pltpu.VMEM((n_off, *held), F32),
            pltpu.VMEM(held, F32),
            pltpu.VMEM((n_c, n_off, *held), F32),
            pltpu.VMEM((tile, tile), F32),
            pltpu.VMEM((tile, tile), F32),
            dma((n_load,)),
            dma((n_off,)),
            dma((n_off,)),
            dma((n_c, n_off)),
            dma((n_c, n_off)),
            pltpu.SemaphoreType.REGULAR,
        ],
        compiler_params=pltpu.CompilerParams(
            collective_id=0, has_side_effects=True, vmem_limit_bytes=56 * 2**20
        ),
    )(*operands)

    return pl.pallas_call(
        back_kernel,
        out_shape=(
            jax.ShapeDtypeStruct((tile, tile), F32),
            jax.ShapeDtypeStruct((tile, tile), BF),
        ),
        in_specs=[in_vmem] * 5,
        out_specs=(in_hbm, in_hbm),
        scratch_shapes=[
            pltpu.VMEM((tile, tile), F32),
            pltpu.VMEM((tile, tile), BF),
            dma((2 * (tile // min(MARGIN, 128)),)),
        ],
        compiler_params=pltpu.CompilerParams(vmem_limit_bytes=16 * 2**20),
    )(*kept)


def solution(mesh):
    in_specs = (P("ty", "tx"), P("ty", "tx"), P("ty", "tx"), P("cond", None, None, None, None))
    out_specs = (P("ty", "tx"), P("ty", "tx"))
    return jax.shard_map(
        per_device, mesh=mesh, in_specs=in_specs, out_specs=out_specs, check_vma=False
    )
```

```python
import functools
import math

import jax
import jax.numpy as jnp
import numpy as np
from jax import lax
from jax.experimental import pallas as pl
from jax.experimental.pallas import tpu as pltpu
from jax.sharding import PartitionSpec as P

MARGIN = 128
STEEPNESS = 6.0
THRESHOLD = 0.25
STEP_SIZE = 4.0
LANES = 128
HALF = 16
USED = 7
SLOT = 2 * HALF
SLOTS = LANES // SLOT
WIDE = 64
MESH = pl.DeviceIdType.MESH
BF = jnp.bfloat16
F32 = jnp.float32


def halves(table):
    table = np.asarray(table, np.float32)
    high = table.astype(BF)
    return high, (table - high.astype(np.float32)).astype(BF)


def place(rows, cols, *pieces):
    out = np.zeros((rows, cols))
    for top, left, piece in pieces:
        out[top : top + piece.shape[0], left : left + piece.shape[1]] = piece
    return out


def spread(order):
    return order + order // USED


def trig(positions, top, period):
    turns = np.mod(np.outer(positions, np.arange(top + 1)), period).astype(np.float64)
    angle = turns * (2 * math.pi / period)
    out = np.zeros((len(positions), SLOT))
    out[:, spread(np.arange(top + 1))] = np.cos(angle)
    out[:, HALF + spread(np.arange(top + 1))] = np.sin(angle)
    return out


def make_tables(tile, margin, band):
    top = band // 2
    assert band % 2 == 0 and spread(top) < HALF and tile >= 2 * margin
    length = tile + 2 * margin
    grid = -(-(2 * band - 1) // 16) * 16
    assert grid <= WIDE
    shifted = []
    for step in (-1, 0, 1):
        spots = np.arange(tile) + margin - step * tile
        inside = ((spots >= 0) & (spots < length))[:, None]
        shifted.append(trig(spots, top, length) * inside)
    wave = np.concatenate(shifted, 1)
    fh, fl = halves(wave)
    pad = np.zeros((tile, LANES - 3 * SLOT), fh.dtype)
    fcol = np.concatenate([fh, pad, fl, pad], 1)
    frow = np.concatenate([fh.T, fl.T], 0)

    ec = trig(np.arange(grid), top, grid)
    bh, bl = halves(ec)
    norm = 1.0 / (length * length)
    sh, sl = halves(ec * norm)
    block = place(LANES, SLOTS * WIDE, *((SLOT * j, WIDE * j, ec.T) for j in range(SLOTS)))
    th, tl = halves(block)
    turn = (np.arange(tile) + margin)[:, None] / length - np.arange(grid)[None, :] / grid
    orders = np.arange(1, band)
    interp = (1 + 2 * np.cos(2 * math.pi * turn[:, :, None] * orders).sum(-1)) / grid
    ih, il = halves(interp)
    gap = np.zeros((tile, WIDE - grid), ih.dtype)
    wn = np.concatenate([ih, gap, ih, gap, il, gap, il, gap], 1)
    wt = np.concatenate([ih.T, il.T], 0)

    plus, minus = np.zeros((HALF, band)), np.zeros((HALF, band))
    for m in range(top):
        plus[spread(m), top + m] = 1
    for m in range(1, top + 1):
        minus[spread(m), top - m] = 1
    even, odd = plus + minus, plus - minus
    kl = np.concatenate([even, even, -odd, odd], 0)
    kr = np.stack([
        place(
            band, 2 * LANES,
            (0, SLOT * j, even.T), (0, SLOT * j + HALF, even.T),
            (0, LANES + SLOT * j, -odd.T), (0, LANES + SLOT * j + HALF, odd.T),
        )
        for j in range(SLOTS)
    ])
    front = dict(
        fcol=fcol, frow=frow, kr=kr.astype(BF), kl=kl.astype(BF),
        left=np.concatenate([sh, sh, sl], 1),
        th=th, tl=tl, wt=wt, wn=wn,
        tb=np.concatenate([th.T, tl.T], 1),
        lt=np.concatenate([bh.T, bh.T, bl.T], 1),
    )
    edge, mid = [0, SLOT], [SLOT, 2 * SLOT]
    rows = np.zeros((tile, 6 * SLOT), fh.dtype)
    for lo, hi, cut in ((0, margin, 0), (tile - margin, tile, SLOT)):
        pick = slice(cut, cut + 2 * SLOT)
        rows[lo:hi] = np.concatenate([fh[lo:hi, pick], fh[lo:hi, pick], fl[lo:hi, pick]], 1)
    lo, hi, pick = margin, tile - margin, slice(SLOT, 2 * SLOT)
    rows[lo:hi, : 3 * SLOT] = np.concatenate([fh[lo:hi, pick], fh[lo:hi, pick], fl[lo:hi, pick]], 1)
    back = dict(frow=frow, brow=rows)
    return front, back, grid


def split(x):
    high = x.astype(BF)
    return high, (x - high.astype(F32)).astype(BF)


def mm(a, b):
    return jnp.dot(a, b, preferred_element_type=F32)


def both_sides(rows, high, low, cols):
    n, m = rows.shape[0] // 2, cols.shape[1] // 2
    q = mm(rows, high)
    q = q[:n] + q[n:] + mm(rows[:n], low)
    out = mm(jnp.concatenate(split(q), 0), cols)
    return out[:n, :m] + out[:n, m:] + out[n:, :m]


def roll(x, shift):
    shift = shift % LANES
    return x if shift == 0 else pltpu.roll(x, shift, 1)


def by_slot(pieces):
    lane = lax.broadcasted_iota(jnp.int32, pieces[0].shape, 1)
    out = pieces[-1]
    for j in range(len(pieces) - 2, -1, -1):
        out = jnp.where(lane < (j + 1) * SLOT, pieces[j], out)
    return out


def swap(x):
    return jnp.concatenate([x[HALF:], x[:HALF]], 0)


def neighbours(ty, tx, n_ty, n_tx):
    here = (0, None, 0)
    if n_ty == 2:
        vert = [here, (1 - 2 * ty, None, 1)]
    else:
        vert = [here, (-1, ty > 0, 2), (1, ty < n_ty - 1, 1)][: 1 if n_ty == 1 else 3]
    side = [here, (1, tx < n_tx - 1, 2), (-1, tx > 0, 1)]
    spots = [(v, h) for v in range(len(vert)) for h in range(len(side))]

    def groups(mirror):
        out = {}
        for v, h in spots:
            keys = (vert[v][2], side[h][2]) if mirror else (v, h)
            key = (keys[0] if vert[v][1] is not None else 0, keys[1])
            out.setdefault(key, []).append((v, h))
        for (v, h), members in reversed(out.items()):
            tests = [t for t in (vert[v][1], side[h][1]) if t is not None]
            ok = None if not tests else tests[0] if len(tests) == 1 else tests[0] & tests[1]
            yield ok, members[::-1]

    return vert, side, spots, groups


def front_kernel(names, grid, n_k, *refs):
    n_tab = len(names)
    logits_hbm, target_hbm, weight_hbm, kern_hbm = refs[:4]
    tab_hbm = dict(zip(names, refs[4 : 4 + n_tab]))
    late_hbm = refs[4 + n_tab]
    out_ref, logits, fac, frow, late = refs[5 + n_tab : 10 + n_tab]
    rest = refs[10 + n_tab :]
    target, weight, kern = rest[:3]
    own = [n for n in names if n != "frow"]
    tab = dict(zip(own, rest[3 : 3 + len(own)]), frow=frow)
    (kq, send1, recv1, zs_own, recv2, level, signed,
     load_sem, s1, r1, s2, r2, ready) = rest[3 + len(own) :]

    tile = logits.shape[0]
    band = kern.shape[-1]
    n_g = n_k // SLOTS
    length = tile + 2 * MARGIN
    norm = 1.0 / (length * length)
    chunk = tile // 4
    parts = [slice(i, i + chunk) for i in range(0, tile, chunk)]
    n_ty, n_tx, n_c = lax.axis_size("ty"), lax.axis_size("tx"), lax.axis_size("cond")
    ty, tx, me = lax.axis_index("ty"), lax.axis_index("tx"), lax.axis_index("cond")

    vert, side, spots, groups = neighbours(ty, tx, n_ty, n_tx)

    def target_of(spot, turn=0):
        v, h = spot
        where = {"ty": ty + vert[v][0], "tx": tx + side[h][0]}
        away = not isinstance(turn, int) or turn
        return dict(where, cond=lax.rem(me + turn, n_c)) if away else where

    def each(mirror, turns, act):
        for ok, members in groups(mirror):
            jobs_here = [(m, t) for m in members for t in turns if m != (0, 0) or not isinstance(t, int) or t]

            def run(jobs_here=jobs_here):
                for spot, turn in jobs_here:
                    act(spot, turn)

            if not jobs_here:
                continue
            if ok is None:
                run()
            else:
                pl.when(ok)(run)

    barrier = pltpu.get_barrier_semaphore()
    def greet(turns):
        each(False, turns, lambda spot, turn: pl.semaphore_signal(
            barrier, inc=1, device_id=target_of(spot, turn), device_id_type=MESH
        ))

    jobs = [(part.start, logits_hbm.at[part], logits.at[part]) for part in parts]
    jobs += [("frow", tab_hbm["frow"], frow), ("fcol", tab_hbm["fcol"], tab["fcol"]), ("kern", kern_hbm, kern)]
    jobs += [(n, tab_hbm[n], tab[n]) for n in ("kr", "kl")]
    jobs += [("target", target_hbm, target), ("weight", weight_hbm, weight)]
    jobs += [(n, tab_hbm[n], tab[n]) for n in own if n not in ("fcol", "kr", "kl")]
    jobs += [("late", late_hbm, late)]
    loads = {}
    for i, (name, source, dest) in enumerate(jobs):
        loads[name] = pltpu.make_async_copy(source, dest, load_sem.at[i])
        loads[name].start()
        if name == "fcol":
            greet((0,))

    for turn in range(1, n_c):
        pl.when(me + turn < n_c)(functools.partial(greet, (turn,)))
    for ok, members in groups(True):
        if ok is None:
            continue

        @pl.when(jnp.logical_not(ok))
        def _():
            for spot in members:
                recv1[spots.index(spot)] = jnp.zeros(recv1.shape[1:], F32)
                for turn in range(n_c):
                    recv2[turn, spots.index(spot)] = jnp.zeros(recv2.shape[2:], F32)

    loads["fcol"].wait()
    for part in parts:
        loads[part.start].wait()
    loads["frow"].wait()
    share = both_sides(frow[...], *split(0.5 + 0.5 * jnp.tanh(logits[...])), tab["fcol"][...])
    strips = {0: share[SLOT : 2 * SLOT]}
    for v in range(1, len(vert)):
        above, below = share[:SLOT], share[2 * SLOT :]
        dr = vert[v][0]
        strips[v] = (above if dr < 0 else below) if isinstance(dr, int) else jnp.where(dr < 0, above, below)
    for i, (v, h) in enumerate(spots):
        send1[i] = by_slot(
            [roll(strips[v][8 * t : 8 * t + 8], SLOT * (t - side[h][0] - 1)) for t in range(SLOTS)]
        )[:USED]

    plane = 0
    for ok, members in groups(True):
        plane = plane + len(members) * (1 if ok is None else ok.astype(jnp.int32))
    pl.semaphore_wait(barrier, plane - 1 + plane * me)

    def first(spot, turn=0):
        i = spots.index(spot)
        return pltpu.make_async_remote_copy(
            src_ref=send1.at[i], dst_ref=recv1.at[i], send_sem=s1.at[i], recv_sem=r1.at[i],
            device_id=target_of(spot), device_id_type=MESH,
        )

    def second(spot, turn):
        i = spots.index(spot)
        return pltpu.make_async_remote_copy(
            src_ref=zs_own, dst_ref=recv2.at[turn, i], send_sem=s2.at[turn, i],
            recv_sem=r2.at[turn, i], device_id=target_of(spot, turn), device_id_type=MESH,
        )

    each(False, (0,), lambda spot, turn: first(spot).start())

    def answer(turn):
        each(False, (turn,), lambda spot, turn: pl.semaphore_signal(
            ready, inc=1, device_id=target_of(spot, turn), device_id_type=MESH
        ))

    for back in range(1, n_c):
        pl.when(me >= back)(functools.partial(answer, n_c - back))

    for name in ("kern", "kr", "kl"):
        loads[name].wait()
    turned = None
    for j in range(SLOTS):
        rows = jnp.concatenate(
            [kern[0, SLOTS * g + j, ri] for g in range(n_g) for ri in range(2)], 0
        )
        high, low = split(rows)
        piece = mm(high, tab["kr"][j]) + mm(low, tab["kr"][j])
        turned = piece if turned is None else turned + piece
    for e in range(2 * n_g):
        high, low = split(turned[e * band : (e + 1) * band])
        kq[:, 2 * LANES * e : 2 * LANES * (e + 1)] = mm(tab["kl"][...], high) + mm(tab["kl"][...], low)
    loads["target"].wait()
    loads["weight"].wait()

    def prepare(i, carry):
        part = pl.ds(pl.multiple_of(i * 32, 32), 32)
        vals = weight[part].astype(F32)
        level[part] = vals
        signed[part] = vals * (2.0 * target[part].astype(F32) - 1.0)
        mask = jnp.tanh(logits[part])
        fac[part] = (1.5 * STEP_SIZE * norm) * (mask * mask - 1.0)
        return carry

    lax.fori_loop(0, tile // 32, prepare, 0)
    for name in own:
        if name not in ("fcol", "kr", "kl"):
            loads[name].wait()
    loads["late"].wait()

    each(False, (0,), lambda spot, turn: first(spot).wait_send())
    each(True, (0,), lambda spot, turn: first(spot).wait_recv())
    spec = send1[0]
    for i in range(1, len(spots)):
        spec = spec + recv1[i]
    rest8 = jnp.zeros((8 - USED, LANES), F32)
    spec = jnp.concatenate([spec, rest8], 0)

    turns = [roll(spec, SLOT * s) for s in range(SLOTS)]
    u = jnp.concatenate(
        [by_slot([turns[(j - t) % SLOTS] for j in range(SLOTS)]) for t in range(SLOTS)], 0
    )
    v = roll(u, HALF)
    us, vs = swap(u), swap(v)

    def quarter(e, row, col):
        left = 2 * LANES * e + LANES * col
        return kq[SLOT * row : SLOT * (row + 1), left : left + LANES]

    coef = []
    for g in range(n_g):
        r, i = 2 * g, 2 * g + 1
        coef.append(quarter(r, 0, 0) * u - quarter(r, 1, 1) * vs - quarter(i, 1, 0) * us - quarter(i, 0, 1) * v)
        coef.append(quarter(i, 0, 0) * u - quarter(i, 1, 1) * vs + quarter(r, 1, 0) * us + quarter(r, 0, 1) * v)
    n_e = 2 * n_g
    ah, al = split(jnp.concatenate(coef, 1))
    half = mm(tab["left"][...], jnp.concatenate([ah, al, ah], 0))
    hh, hl = split(jnp.concatenate([half[:, LANES * e : LANES * (e + 1)] for e in range(n_e)], 0))
    th, tl = tab["th"][...], tab["tl"][...]
    field = mm(jnp.concatenate([hh, hl, hh], 1), jnp.concatenate([th, th, tl], 0))
    coarse = jnp.zeros((grid, 2 * LANES), F32)
    for e in range(n_e):
        cut = field[grid * e : grid * (e + 1)]
        coarse = coarse + cut * cut
    coarse = coarse[:, :LANES] + coarse[:, LANES:]
    lane = lax.broadcasted_iota(jnp.int32, coarse.shape, 1)
    coarse = (0.5 * STEEPNESS) * (coarse - jnp.where(lane < WIDE, THRESHOLD, 0.0))
    ch, cl = split(coarse)
    wt = tab["wt"]
    hole = jnp.zeros((WIDE - grid, tile), BF)
    wth, wtl = [wt[:grid], hole] * 2, [wt[grid:], hole] * 2
    uh, ul = split(mm(jnp.concatenate([ch, cl, ch], 1), jnp.concatenate(wth + wth + wtl, 0)))
    gap = jnp.zeros((WIDE - grid, tile), BF)
    ustack = jnp.concatenate([uh, gap, ul, gap, uh, gap, gap, gap, gap, gap], 0)[: 4 * WIDE]

    th = jnp.tanh(mm(tab["wn"][...], ustack))
    gain = (level[...] * th - signed[...]) * (1.0 - th * th)
    gcoarse = both_sides(wt[...], *split(gain), tab["wn"][...])

    gpair = jnp.concatenate([gcoarse, gcoarse], 1)
    dh, dl = split(jnp.concatenate([gpair * field[grid * e : grid * (e + 1)] for e in range(n_e)], 0))
    wide = mm(dh, tab["tb"][...])
    down = wide[:, :LANES] + wide[:, LANES:] + mm(dl, tab["tb"][:, :LANES])
    eh, el = split(jnp.concatenate([down[grid * e : grid * (e + 1)] for e in range(n_e)], 1))
    d = mm(tab["lt"][...], jnp.concatenate([eh, el, eh], 0))
    du = jnp.zeros((SLOT, LANES), F32)
    dus, dv, dvs = du, du, du
    for g in range(n_g):
        r, i = 2 * g, 2 * g + 1
        dr_, di_ = d[:, LANES * r : LANES * (r + 1)], d[:, LANES * i : LANES * (i + 1)]
        du = du + quarter(r, 0, 0) * dr_ + quarter(i, 0, 0) * di_
        dus = dus + quarter(r, 1, 0) * di_ - quarter(i, 1, 0) * dr_
        dv = dv + quarter(r, 0, 1) * di_ - quarter(i, 0, 1) * dr_
        dvs = dvs - quarter(r, 1, 1) * dr_ - quarter(i, 1, 1) * di_
    dx = du + swap(dus) + roll(dv + swap(dvs), HALF)
    x = [dx[8 * t : 8 * t + 8] for t in range(SLOTS)]
    lane = lax.broadcasted_iota(jnp.int32, (8, LANES), 1)
    even, low = (lane // SLOT) % 2 == 0, lane < 2 * SLOT
    pair = [
        jnp.where(even, a, b) + jnp.where(
            even, roll(jnp.where(even, b, a), -SLOT), roll(jnp.where(even, b, a), SLOT)
        )
        for a, b in ((x[0], x[1]), (x[2], x[3]))
    ]
    zs = jnp.where(low, pair[0], pair[1]) + roll(jnp.where(low, pair[1], pair[0]), 2 * SLOT)
    zs_own[...] = zs[:USED]

    @pl.when(me < n_c - 1)
    def _():
        pl.semaphore_wait(ready, plane * (n_c - 1 - me))

    high = (2 * me >= n_c).astype(jnp.int32)
    for k in range(n_c - 1):
        up = k + (k >= me).astype(jnp.int32)
        down = n_c - 1 - k - (n_c - 1 - k <= me).astype(jnp.int32)
        goal = high * up + (1 - high) * down
        turn = lax.rem(goal - me + n_c, n_c)
        each(False, (turn,), lambda spot, turn: second(spot, turn).start())
    each(False, (0,), lambda spot, turn: second(spot, turn).start())
    recv2[0, 0] = zs_own[...]
    each(False, range(n_c), lambda spot, turn: second(spot, turn).wait_send())
    totals = None
    for turn in range(n_c):
        each(True, (turn,), lambda spot, turn: second(spot, turn).wait_recv())
        came = [recv2[turn, i] for i in range(len(spots))]
        totals = came if totals is None else [a + b for a, b in zip(totals, came)]
    blocks = {spot: jnp.concatenate([t, rest8], 0) for spot, t in zip(spots, totals)}
    bands = []
    for v in range(len(vert)):
        line = [blocks[v, h] for h in (1, 0, 2)]
        bands.append(jnp.concatenate(
            [by_slot([roll(b, SLOT * (i - t)) for i, b in enumerate(line)]) for t in range(SLOTS)], 0
        ))
    none = jnp.zeros((SLOT, LANES), F32)
    if len(vert) == 1:
        above = below = none
    elif len(vert) == 2:
        above = jnp.where(vert[1][0] < 0, bands[1], none)
        below = jnp.where(vert[1][0] < 0, none, bands[1])
    else:
        above, below = bands[2], bands[1]
    out_ref[:SLOT] = above
    out_ref[SLOT : 2 * SLOT] = bands[0]
    out_ref[2 * SLOT :] = below


def back_kernel(z_ref, logits, fac, frow, brow, new_hbm, next_hbm, new, nxt, sem):
    tile = logits.shape[1]
    n_f = 3 * SLOT
    zh, zl = split(z_ref[:, :n_f])
    w = mm(zh, frow[:n_f]) + mm(zl, frow[:n_f]) + mm(zh, frow[n_f:])
    wh, wl = split(w)

    chunk = min(MARGIN, 128)
    copies = []
    for i in range(tile // chunk):
        lo, hi = i * chunk, (i + 1) * chunk
        part = slice(lo, hi)
        first = 0 if lo < MARGIN else SLOT
        last = 3 * SLOT if hi > tile - MARGIN else 2 * SLOT
        pick = slice(first, last)
        stack = jnp.concatenate([wh[pick], wl[pick], wh[pick]], 0)
        grad = mm(brow[part, : 3 * (last - first)], stack)
        value = logits[part] + fac[part] * grad
        new[part] = value
        nxt[part] = (0.5 + 0.5 * jnp.tanh(value)).astype(BF)
        for j, (buf, out) in enumerate(((new, new_hbm), (nxt, next_hbm))):
            copy = pltpu.make_async_copy(buf.at[part], out.at[part], sem.at[2 * i + j])
            copy.start()
            copies.append(copy)
    for copy in copies:
        copy.wait()


def per_device(mask_logits, target_layout, density_weights, socs_kernels):
    tile = mask_logits.shape[0]
    band = socs_kernels.shape[-1]
    n_k = socs_kernels.shape[1]
    assert n_k % SLOTS == 0
    n_c, n_ty = lax.axis_size("cond"), lax.axis_size("ty")
    front, back, grid = make_tables(tile, MARGIN, band)
    names = list(front)
    arrays = [mask_logits, target_layout, density_weights, socs_kernels]
    tables = {n: jnp.asarray(front[n]) for n in names}
    late = jnp.asarray(back["brow"])
    in_vmem = pl.BlockSpec(memory_space=pltpu.VMEM)
    in_hbm = pl.BlockSpec(memory_space=pl.ANY)
    vmem = lambda a: pltpu.VMEM(a.shape, a.dtype)
    dma = pltpu.SemaphoreType.DMA
    n_off = 3 * min(n_ty, 3)
    held = (USED, LANES)
    n_load = len(names) + 5 + 4
    operands = arrays + [tables[n] for n in names] + [late]
    kept = pl.pallas_call(
        functools.partial(front_kernel, names, grid, n_k),
        out_shape=[
            pltpu.VMEM((3 * SLOT, LANES), F32), pltpu.VMEM((tile, tile), F32),
            pltpu.VMEM((tile, tile), F32), vmem(tables["frow"]), vmem(late),
        ],
        in_specs=[in_hbm] * len(operands),
        out_specs=[in_vmem] * 5,
        scratch_shapes=[vmem(a) for a in arrays[1:]]
        + [vmem(tables[n]) for n in names if n != "frow"]
        + [
            pltpu.VMEM((2 * SLOT, 2 * LANES * 2 * n_k // SLOTS), F32),
            pltpu.VMEM((n_off, *held), F32),
            pltpu.VMEM((n_off, *held), F32),
            pltpu.VMEM(held, F32),
            pltpu.VMEM((n_c, n_off, *held), F32),
            pltpu.VMEM((tile, tile), F32),
            pltpu.VMEM((tile, tile), F32),
            dma((n_load,)),
            dma((n_off,)),
            dma((n_off,)),
            dma((n_c, n_off)),
            dma((n_c, n_off)),
            pltpu.SemaphoreType.REGULAR,
        ],
        compiler_params=pltpu.CompilerParams(
            collective_id=0, has_side_effects=True, vmem_limit_bytes=56 * 2**20
        ),
    )(*operands)

    return pl.pallas_call(
        back_kernel,
        out_shape=(
            jax.ShapeDtypeStruct((tile, tile), F32),
            jax.ShapeDtypeStruct((tile, tile), BF),
        ),
        in_specs=[in_vmem] * 5,
        out_specs=(in_hbm, in_hbm),
        scratch_shapes=[
            pltpu.VMEM((tile, tile), F32),
            pltpu.VMEM((tile, tile), BF),
            dma((2 * (tile // min(MARGIN, 128)),)),
        ],
        compiler_params=pltpu.CompilerParams(vmem_limit_bytes=16 * 2**20),
    )(*kept)


def solution(mesh):
    in_specs = (P("ty", "tx"), P("ty", "tx"), P("ty", "tx"), P("cond", None, None, None, None))
    out_specs = (P("ty", "tx"), P("ty", "tx"))
    return jax.shard_map(
        per_device, mesh=mesh, in_specs=in_specs, out_specs=out_specs, check_vma=False
    )
```

```python
import functools
import math

import jax
import jax.numpy as jnp
import numpy as np
from jax import lax
from jax.experimental import pallas as pl
from jax.experimental.pallas import tpu as pltpu
from jax.sharding import PartitionSpec as P

MARGIN = 128
STEEPNESS = 6.0
THRESHOLD = 0.25
STEP_SIZE = 4.0
LANES = 128
HALF = 16
USED = 7
SLOT = 2 * HALF
SLOTS = LANES // SLOT
WIDE = 64
MESH = pl.DeviceIdType.MESH
BF = jnp.bfloat16
F32 = jnp.float32


def halves(table):
    table = np.asarray(table, np.float32)
    high = table.astype(BF)
    return high, (table - high.astype(np.float32)).astype(BF)


def place(rows, cols, *pieces):
    out = np.zeros((rows, cols))
    for top, left, piece in pieces:
        out[top : top + piece.shape[0], left : left + piece.shape[1]] = piece
    return out


def spread(order):
    return order + order // USED


def trig(positions, top, period):
    turns = np.mod(np.outer(positions, np.arange(top + 1)), period).astype(np.float64)
    angle = turns * (2 * math.pi / period)
    out = np.zeros((len(positions), SLOT))
    out[:, spread(np.arange(top + 1))] = np.cos(angle)
    out[:, HALF + spread(np.arange(top + 1))] = np.sin(angle)
    return out


def make_tables(tile, margin, band):
    top = band // 2
    assert band % 2 == 0 and spread(top) < HALF and tile >= 2 * margin
    length = tile + 2 * margin
    grid = -(-(2 * band - 1) // 16) * 16
    assert grid <= WIDE
    shifted = []
    for step in (-1, 0, 1):
        spots = np.arange(tile) + margin - step * tile
        inside = ((spots >= 0) & (spots < length))[:, None]
        shifted.append(trig(spots, top, length) * inside)
    wave = np.concatenate(shifted, 1)
    fh, fl = halves(wave)
    pad = np.zeros((tile, LANES - 3 * SLOT), fh.dtype)
    fcol = np.concatenate([fh, pad, fl, pad], 1)
    frow = np.concatenate([fh.T, fl.T], 0)

    ec = trig(np.arange(grid), top, grid)
    bh, bl = halves(ec)
    norm = 1.0 / (length * length)
    sh, sl = halves(ec * norm)
    block = place(LANES, SLOTS * WIDE, *((SLOT * j, WIDE * j, ec.T) for j in range(SLOTS)))
    th, tl = halves(block)
    turn = (np.arange(tile) + margin)[:, None] / length - np.arange(grid)[None, :] / grid
    orders = np.arange(1, band)
    interp = (1 + 2 * np.cos(2 * math.pi * turn[:, :, None] * orders).sum(-1)) / grid
    ih, il = halves(interp)
    gap = np.zeros((tile, WIDE - grid), ih.dtype)
    wn = np.concatenate([ih, gap, ih, gap, il, gap, il, gap], 1)
    wt = np.concatenate([ih.T, il.T], 0)

    plus, minus = np.zeros((HALF, band)), np.zeros((HALF, band))
    for m in range(top):
        plus[spread(m), top + m] = 1
    for m in range(1, top + 1):
        minus[spread(m), top - m] = 1
    even, odd = plus + minus, plus - minus
    kl = np.concatenate([even, even, -odd, odd], 0)
    kr = np.stack([
        place(
            band, 2 * LANES,
            (0, SLOT * j, even.T), (0, SLOT * j + HALF, even.T),
            (0, LANES + SLOT * j, -odd.T), (0, LANES + SLOT * j + HALF, odd.T),
        )
        for j in range(SLOTS)
    ])
    total = wave.sum(0)
    flat = place(3 * SLOT, LANES, (0, 0, 0.5 * np.outer(total, total))).astype(np.float32)
    front = dict(
        flat=flat, fcol=fcol, frow=frow, kr=kr.astype(BF), kl=kl.astype(BF),
        left=np.concatenate([sh, sh, sl], 1),
        th=th, tl=tl, wt=wt, wn=wn,
        tb=np.concatenate([th.T, tl.T], 1),
        lt=np.concatenate([bh.T, bh.T, bl.T], 1),
    )
    edge, mid = [0, SLOT], [SLOT, 2 * SLOT]
    rows = np.zeros((tile, 6 * SLOT), fh.dtype)
    for lo, hi, cut in ((0, margin, 0), (tile - margin, tile, SLOT)):
        pick = slice(cut, cut + 2 * SLOT)
        rows[lo:hi] = np.concatenate([fh[lo:hi, pick], fh[lo:hi, pick], fl[lo:hi, pick]], 1)
    lo, hi, pick = margin, tile - margin, slice(SLOT, 2 * SLOT)
    rows[lo:hi, : 3 * SLOT] = np.concatenate([fh[lo:hi, pick], fh[lo:hi, pick], fl[lo:hi, pick]], 1)
    back = dict(frow=frow, brow=rows)
    return front, back, grid


def split(x):
    high = x.astype(BF)
    return high, (x - high.astype(F32)).astype(BF)


def mm(a, b):
    return jnp.dot(a, b, preferred_element_type=F32)


def both_sides(rows, high, low, cols):
    n, m = rows.shape[0] // 2, cols.shape[1] // 2
    q = mm(rows, high)
    q = q[:n] + q[n:] + mm(rows[:n], low)
    out = mm(jnp.concatenate(split(q), 0), cols)
    return out[:n, :m] + out[:n, m:] + out[n:, :m]


def roll(x, shift):
    shift = shift % LANES
    return x if shift == 0 else pltpu.roll(x, shift, 1)


def by_slot(pieces):
    lane = lax.broadcasted_iota(jnp.int32, pieces[0].shape, 1)
    out = pieces[-1]
    for j in range(len(pieces) - 2, -1, -1):
        out = jnp.where(lane < (j + 1) * SLOT, pieces[j], out)
    return out


def swap(x):
    return jnp.concatenate([x[HALF:], x[:HALF]], 0)


def neighbours(ty, tx, n_ty, n_tx):
    here = (0, None, 0)
    if n_ty == 2:
        vert = [here, (1 - 2 * ty, None, 1)]
    else:
        vert = [here, (-1, ty > 0, 2), (1, ty < n_ty - 1, 1)][: 1 if n_ty == 1 else 3]
    side = [here, (1, tx < n_tx - 1, 2), (-1, tx > 0, 1)]
    spots = [(v, h) for v in range(len(vert)) for h in range(len(side))]

    def groups(mirror):
        out = {}
        for v, h in spots:
            keys = (vert[v][2], side[h][2]) if mirror else (v, h)
            key = (keys[0] if vert[v][1] is not None else 0, keys[1])
            out.setdefault(key, []).append((v, h))
        for (v, h), members in reversed(out.items()):
            tests = [t for t in (vert[v][1], side[h][1]) if t is not None]
            ok = None if not tests else tests[0] if len(tests) == 1 else tests[0] & tests[1]
            yield ok, members[::-1]

    return vert, side, spots, groups


def front_kernel(names, grid, n_k, *refs):
    n_tab = len(names)
    logits_hbm, target_hbm, weight_hbm, kern_hbm = refs[:4]
    tab_hbm = dict(zip(names, refs[4 : 4 + n_tab]))
    late_hbm = refs[4 + n_tab]
    out_ref, logits, fac, frow, late = refs[5 + n_tab : 10 + n_tab]
    rest = refs[10 + n_tab :]
    target, weight, kern = rest[:3]
    own = [n for n in names if n != "frow"]
    tab = dict(zip(own, rest[3 : 3 + len(own)]), frow=frow)
    (kq, send1, recv1, zs_own, recv2, level, signed,
     load_sem, s1, r1, s2, r2, ready) = rest[3 + len(own) :]

    tile = logits.shape[0]
    band = kern.shape[-1]
    n_g = n_k // SLOTS
    length = tile + 2 * MARGIN
    norm = 1.0 / (length * length)
    chunk = tile // 4
    parts = [slice(i, i + chunk) for i in range(0, tile, chunk)]
    n_ty, n_tx, n_c = lax.axis_size("ty"), lax.axis_size("tx"), lax.axis_size("cond")
    ty, tx, me = lax.axis_index("ty"), lax.axis_index("tx"), lax.axis_index("cond")

    vert, side, spots, groups = neighbours(ty, tx, n_ty, n_tx)

    def target_of(spot, turn=0):
        v, h = spot
        where = {"ty": ty + vert[v][0], "tx": tx + side[h][0]}
        away = not isinstance(turn, int) or turn
        return dict(where, cond=lax.rem(me + turn, n_c)) if away else where

    def each(mirror, turns, act):
        for ok, members in groups(mirror):
            jobs_here = [(m, t) for m in members for t in turns if m != (0, 0) or not isinstance(t, int) or t]

            def run(jobs_here=jobs_here):
                for spot, turn in jobs_here:
                    act(spot, turn)

            if not jobs_here:
                continue
            if ok is None:
                run()
            else:
                pl.when(ok)(run)

    barrier = pltpu.get_barrier_semaphore()
    def greet(turns):
        each(False, turns, lambda spot, turn: pl.semaphore_signal(
            barrier, inc=1, device_id=target_of(spot, turn), device_id_type=MESH
        ))

    jobs = [(part.start, logits_hbm.at[part], logits.at[part]) for part in parts]
    jobs += [("frow", tab_hbm["frow"], frow), ("fcol", tab_hbm["fcol"], tab["fcol"]), ("flat", tab_hbm["flat"], tab["flat"]), ("kern", kern_hbm, kern)]
    jobs += [(n, tab_hbm[n], tab[n]) for n in ("kr", "kl")]
    jobs += [("target", target_hbm, target), ("weight", weight_hbm, weight)]
    jobs += [(n, tab_hbm[n], tab[n]) for n in own if n not in ("fcol", "flat", "kr", "kl")]
    jobs += [("late", late_hbm, late)]
    loads = {}
    for i, (name, source, dest) in enumerate(jobs):
        loads[name] = pltpu.make_async_copy(source, dest, load_sem.at[i])
        loads[name].start()
        if name == "fcol":
            greet((0,))

    for turn in range(1, n_c):
        pl.when(me + turn < n_c)(functools.partial(greet, (turn,)))
    for ok, members in groups(True):
        if ok is None:
            continue

        @pl.when(jnp.logical_not(ok))
        def _():
            for spot in members:
                recv1[spots.index(spot)] = jnp.zeros(recv1.shape[1:], F32)
                for turn in range(n_c):
                    recv2[turn, spots.index(spot)] = jnp.zeros(recv2.shape[2:], F32)

    loads["fcol"].wait()
    for part in parts:
        loads[part.start].wait()
    loads["frow"].wait()
    loads["flat"].wait()
    share = both_sides(frow[...], *split(jnp.tanh(logits[...])), tab["fcol"][...])
    share = 0.5 * share + tab["flat"][...]
    strips = {0: share[SLOT : 2 * SLOT]}
    for v in range(1, len(vert)):
        above, below = share[:SLOT], share[2 * SLOT :]
        dr = vert[v][0]
        strips[v] = (above if dr < 0 else below) if isinstance(dr, int) else jnp.where(dr < 0, above, below)
    for i, (v, h) in enumerate(spots):
        send1[i] = by_slot(
            [roll(strips[v][8 * t : 8 * t + 8], SLOT * (t - side[h][0] - 1)) for t in range(SLOTS)]
        )[:USED]

    plane = 0
    for ok, members in groups(True):
        plane = plane + len(members) * (1 if ok is None else ok.astype(jnp.int32))
    pl.semaphore_wait(barrier, plane - 1 + plane * me)

    def first(spot, turn=0):
        i = spots.index(spot)
        return pltpu.make_async_remote_copy(
            src_ref=send1.at[i], dst_ref=recv1.at[i], send_sem=s1.at[i], recv_sem=r1.at[i],
            device_id=target_of(spot), device_id_type=MESH,
        )

    def second(spot, turn):
        i = spots.index(spot)
        return pltpu.make_async_remote_copy(
            src_ref=zs_own, dst_ref=recv2.at[turn, i], send_sem=s2.at[turn, i],
            recv_sem=r2.at[turn, i], device_id=target_of(spot, turn), device_id_type=MESH,
        )

    each(False, (0,), lambda spot, turn: first(spot).start())

    def answer(turn):
        each(False, (turn,), lambda spot, turn: pl.semaphore_signal(
            ready, inc=1, device_id=target_of(spot, turn), device_id_type=MESH
        ))

    for back in range(1, n_c):
        pl.when(me >= back)(functools.partial(answer, n_c - back))

    for name in ("kern", "kr", "kl"):
        loads[name].wait()
    turned = None
    for j in range(SLOTS):
        rows = jnp.concatenate(
            [kern[0, SLOTS * g + j, ri] for g in range(n_g) for ri in range(2)], 0
        )
        high, low = split(rows)
        piece = mm(high, tab["kr"][j]) + mm(low, tab["kr"][j])
        turned = piece if turned is None else turned + piece
    for e in range(2 * n_g):
        high, low = split(turned[e * band : (e + 1) * band])
        kq[:, 2 * LANES * e : 2 * LANES * (e + 1)] = mm(tab["kl"][...], high) + mm(tab["kl"][...], low)
    loads["target"].wait()
    loads["weight"].wait()

    def prepare(i, carry):
        part = pl.ds(pl.multiple_of(i * 32, 32), 32)
        vals = weight[part].astype(F32)
        level[part] = vals
        signed[part] = vals * (2.0 * target[part].astype(F32) - 1.0)
        mask = jnp.tanh(logits[part])
        fac[part] = (1.5 * STEP_SIZE * norm) * (mask * mask - 1.0)
        return carry

    lax.fori_loop(0, tile // 32, prepare, 0)
    for name in own:
        if name not in ("fcol", "flat", "kr", "kl"):
            loads[name].wait()
    loads["late"].wait()

    each(False, (0,), lambda spot, turn: first(spot).wait_send())
    each(True, (0,), lambda spot, turn: first(spot).wait_recv())
    spec = send1[0]
    for i in range(1, len(spots)):
        spec = spec + recv1[i]
    rest8 = jnp.zeros((8 - USED, LANES), F32)
    spec = jnp.concatenate([spec, rest8], 0)

    turns = [roll(spec, SLOT * s) for s in range(SLOTS)]
    u = jnp.concatenate(
        [by_slot([turns[(j - t) % SLOTS] for j in range(SLOTS)]) for t in range(SLOTS)], 0
    )
    v = roll(u, HALF)
    us, vs = swap(u), swap(v)

    def quarter(e, row, col):
        left = 2 * LANES * e + LANES * col
        return kq[SLOT * row : SLOT * (row + 1), left : left + LANES]

    coef = []
    for g in range(n_g):
        r, i = 2 * g, 2 * g + 1
        coef.append(quarter(r, 0, 0) * u - quarter(r, 1, 1) * vs - quarter(i, 1, 0) * us - quarter(i, 0, 1) * v)
        coef.append(quarter(i, 0, 0) * u - quarter(i, 1, 1) * vs + quarter(r, 1, 0) * us + quarter(r, 0, 1) * v)
    n_e = 2 * n_g
    ah, al = split(jnp.concatenate(coef, 1))
    half = mm(tab["left"][...], jnp.concatenate([ah, al, ah], 0))
    hh, hl = split(jnp.concatenate([half[:, LANES * e : LANES * (e + 1)] for e in range(n_e)], 0))
    th, tl = tab["th"][...], tab["tl"][...]
    field = mm(jnp.concatenate([hh, hl, hh], 1), jnp.concatenate([th, th, tl], 0))
    coarse = jnp.zeros((grid, 2 * LANES), F32)
    for e in range(n_e):
        cut = field[grid * e : grid * (e + 1)]
        coarse = coarse + cut * cut
    coarse = coarse[:, :LANES] + coarse[:, LANES:]
    lane = lax.broadcasted_iota(jnp.int32, coarse.shape, 1)
    coarse = (0.5 * STEEPNESS) * (coarse - jnp.where(lane < WIDE, THRESHOLD, 0.0))
    ch, cl = split(coarse)
    wt = tab["wt"]
    hole = jnp.zeros((WIDE - grid, tile), BF)
    wth, wtl = [wt[:grid], hole] * 2, [wt[grid:], hole] * 2
    uh, ul = split(mm(jnp.concatenate([ch, cl, ch], 1), jnp.concatenate(wth + wth + wtl, 0)))
    gap = jnp.zeros((WIDE - grid, tile), BF)
    ustack = jnp.concatenate([uh, gap, ul, gap, uh, gap, gap, gap, gap, gap], 0)[: 4 * WIDE]

    th = jnp.tanh(mm(tab["wn"][...], ustack))
    gain = (level[...] * th - signed[...]) * (1.0 - th * th)
    gcoarse = both_sides(wt[...], *split(gain), tab["wn"][...])

    gpair = jnp.concatenate([gcoarse, gcoarse], 1)
    dh, dl = split(jnp.concatenate([gpair * field[grid * e : grid * (e + 1)] for e in range(n_e)], 0))
    wide = mm(dh, tab["tb"][...])
    down = wide[:, :LANES] + wide[:, LANES:] + mm(dl, tab["tb"][:, :LANES])
    eh, el = split(jnp.concatenate([down[grid * e : grid * (e + 1)] for e in range(n_e)], 1))
    d = mm(tab["lt"][...], jnp.concatenate([eh, el, eh], 0))
    du = jnp.zeros((SLOT, LANES), F32)
    dus, dv, dvs = du, du, du
    for g in range(n_g):
        r, i = 2 * g, 2 * g + 1
        dr_, di_ = d[:, LANES * r : LANES * (r + 1)], d[:, LANES * i : LANES * (i + 1)]
        du = du + quarter(r, 0, 0) * dr_ + quarter(i, 0, 0) * di_
        dus = dus + quarter(r, 1, 0) * di_ - quarter(i, 1, 0) * dr_
        dv = dv + quarter(r, 0, 1) * di_ - quarter(i, 0, 1) * dr_
        dvs = dvs - quarter(r, 1, 1) * dr_ - quarter(i, 1, 1) * di_
    dx = du + swap(dus) + roll(dv + swap(dvs), HALF)
    x = [dx[8 * t : 8 * t + 8] for t in range(SLOTS)]
    lane = lax.broadcasted_iota(jnp.int32, (8, LANES), 1)
    even, low = (lane // SLOT) % 2 == 0, lane < 2 * SLOT
    pair = [
        jnp.where(even, a, b) + jnp.where(
            even, roll(jnp.where(even, b, a), -SLOT), roll(jnp.where(even, b, a), SLOT)
        )
        for a, b in ((x[0], x[1]), (x[2], x[3]))
    ]
    zs = jnp.where(low, pair[0], pair[1]) + roll(jnp.where(low, pair[1], pair[0]), 2 * SLOT)
    zs_own[...] = zs[:USED]

    @pl.when(me < n_c - 1)
    def _():
        pl.semaphore_wait(ready, plane * (n_c - 1 - me))

    high = (2 * me >= n_c).astype(jnp.int32)
    for k in range(n_c - 1):
        up = k + (k >= me).astype(jnp.int32)
        down = n_c - 1 - k - (n_c - 1 - k <= me).astype(jnp.int32)
        goal = high * up + (1 - high) * down
        turn = lax.rem(goal - me + n_c, n_c)
        each(False, (turn,), lambda spot, turn: second(spot, turn).start())
    each(False, (0,), lambda spot, turn: second(spot, turn).start())
    recv2[0, 0] = zs_own[...]
    each(False, range(n_c), lambda spot, turn: second(spot, turn).wait_send())
    totals = None
    for turn in range(n_c):
        each(True, (turn,), lambda spot, turn: second(spot, turn).wait_recv())
        came = [recv2[turn, i] for i in range(len(spots))]
        totals = came if totals is None else [a + b for a, b in zip(totals, came)]
    blocks = {spot: jnp.concatenate([t, rest8], 0) for spot, t in zip(spots, totals)}
    bands = []
    for v in range(len(vert)):
        line = [blocks[v, h] for h in (1, 0, 2)]
        bands.append(jnp.concatenate(
            [by_slot([roll(b, SLOT * (i - t)) for i, b in enumerate(line)]) for t in range(SLOTS)], 0
        ))
    none = jnp.zeros((SLOT, LANES), F32)
    if len(vert) == 1:
        above = below = none
    elif len(vert) == 2:
        above = jnp.where(vert[1][0] < 0, bands[1], none)
        below = jnp.where(vert[1][0] < 0, none, bands[1])
    else:
        above, below = bands[2], bands[1]
    out_ref[:SLOT] = above
    out_ref[SLOT : 2 * SLOT] = bands[0]
    out_ref[2 * SLOT :] = below


def back_kernel(z_ref, logits, fac, frow, brow, new_hbm, next_hbm, new, nxt, sem):
    tile = logits.shape[1]
    n_f = 3 * SLOT
    zh, zl = split(z_ref[:, :n_f])
    w = mm(jnp.concatenate([zh, zl], 0), frow[:n_f])
    w = w[:n_f] + w[n_f:] + mm(zh, frow[n_f:])
    wh, wl = split(w)

    chunk = min(MARGIN, 128)
    copies = []
    for i in range(tile // chunk):
        lo, hi = i * chunk, (i + 1) * chunk
        part = slice(lo, hi)
        first = 0 if lo < MARGIN else SLOT
        last = 3 * SLOT if hi > tile - MARGIN else 2 * SLOT
        pick = slice(first, last)
        stack = jnp.concatenate([wh[pick], wl[pick], wh[pick]], 0)
        grad = mm(brow[part, : 3 * (last - first)], stack)
        value = logits[part] + fac[part] * grad
        new[part] = value
        for j, (buf, out) in enumerate(((new, new_hbm), (nxt, next_hbm))):
            if j == 1:
                nxt[part] = (0.5 + 0.5 * jnp.tanh(value)).astype(BF)
            copy = pltpu.make_async_copy(buf.at[part], out.at[part], sem.at[2 * i + j])
            copy.start()
            copies.append(copy)
    for copy in copies:
        copy.wait()


def per_device(mask_logits, target_layout, density_weights, socs_kernels):
    tile = mask_logits.shape[0]
    band = socs_kernels.shape[-1]
    n_k = socs_kernels.shape[1]
    assert n_k % SLOTS == 0
    n_c, n_ty = lax.axis_size("cond"), lax.axis_size("ty")
    front, back, grid = make_tables(tile, MARGIN, band)
    names = list(front)
    arrays = [mask_logits, target_layout, density_weights, socs_kernels]
    tables = {n: jnp.asarray(front[n]) for n in names}
    late = jnp.asarray(back["brow"])
    in_vmem = pl.BlockSpec(memory_space=pltpu.VMEM)
    in_hbm = pl.BlockSpec(memory_space=pl.ANY)
    vmem = lambda a: pltpu.VMEM(a.shape, a.dtype)
    dma = pltpu.SemaphoreType.DMA
    n_off = 3 * min(n_ty, 3)
    held = (USED, LANES)
    n_load = len(names) + 5 + 4
    operands = arrays + [tables[n] for n in names] + [late]
    kept = pl.pallas_call(
        functools.partial(front_kernel, names, grid, n_k),
        out_shape=[
            pltpu.VMEM((3 * SLOT, LANES), F32), pltpu.VMEM((tile, tile), F32),
            pltpu.VMEM((tile, tile), F32), vmem(tables["frow"]), vmem(late),
        ],
        in_specs=[in_hbm] * len(operands),
        out_specs=[in_vmem] * 5,
        scratch_shapes=[vmem(a) for a in arrays[1:]]
        + [vmem(tables[n]) for n in names if n != "frow"]
        + [
            pltpu.VMEM((2 * SLOT, 2 * LANES * 2 * n_k // SLOTS), F32),
            pltpu.VMEM((n_off, *held), F32),
            pltpu.VMEM((n_off, *held), F32),
            pltpu.VMEM(held, F32),
            pltpu.VMEM((n_c, n_off, *held), F32),
            pltpu.VMEM((tile, tile), F32),
            pltpu.VMEM((tile, tile), F32),
            dma((n_load,)),
            dma((n_off,)),
            dma((n_off,)),
            dma((n_c, n_off)),
            dma((n_c, n_off)),
            pltpu.SemaphoreType.REGULAR,
        ],
        compiler_params=pltpu.CompilerParams(
            collective_id=0, has_side_effects=True, vmem_limit_bytes=56 * 2**20
        ),
    )(*operands)

    return pl.pallas_call(
        back_kernel,
        out_shape=(
            jax.ShapeDtypeStruct((tile, tile), F32),
            jax.ShapeDtypeStruct((tile, tile), BF),
        ),
        in_specs=[in_vmem] * 5,
        out_specs=(in_hbm, in_hbm),
        scratch_shapes=[
            pltpu.VMEM((tile, tile), F32),
            pltpu.VMEM((tile, tile), BF),
            dma((2 * (tile // min(MARGIN, 128)),)),
        ],
        compiler_params=pltpu.CompilerParams(vmem_limit_bytes=16 * 2**20),
    )(*kept)


def solution(mesh):
    in_specs = (P("ty", "tx"), P("ty", "tx"), P("ty", "tx"), P("cond", None, None, None, None))
    out_specs = (P("ty", "tx"), P("ty", "tx"))
    return jax.shard_map(
        per_device, mesh=mesh, in_specs=in_specs, out_specs=out_specs, check_vma=False
    )
```
